32 devices in a mesh: groups: 2 (over y), ctx: 4 (over z), head: 4 (over x, core).
Axes of the slice: x: 2, y: 2, z: 4, core: 2. Of those that a mesh axis runs over, the one named last changes fastest.
Arguments:
- queries: bfloat16 [1024, 32, 128], P(('groups', 'ctx'), 'head'), parts along dimension 0, may hold values from -16 to 16
- positions: int32 [1024], P(('groups', 'ctx')), parts along dimension 0, may hold values from 4096 to 6143
- key_codes: bfloat16 [4, 4096, 128], P('groups', 'ctx'), parts along dimension 0, may hold values from -16 to 16
- value_codes: bfloat16 [4, 4096, 128], P('groups', 'ctx'), parts along dimension 0, may hold values from -8 to 8
- scale_index: int32 [4, 2, 32], P('groups', None, 'ctx'), parts along dimension 0, may hold values from 0 to 15
- scale_table: float32 [2, 16], replicated, may hold values from 0.5 to 2
- block_lists: int32 [64, 4, 8], P(('groups', 'head')), parts along dimension 0, may hold values from 0 to 31, as said below
Outputs:
- attended: bfloat16 [1024, 4096], P(('groups', 'ctx', 'head')), parts along dimension 0
The draws below stay inside these ranges and needn't reach their ends.
There are 2 independent parts, one for each index of `groups`. The reference program is written for one: setup_inputs(seed, part) draws one part's arguments, and reference() takes and returns one part's arrays. A program takes and returns all parts, laid end to end along the dimension named above; an argument that names none is the same for every part. Nothing has to cross between parts.
Inputs may be any that keep to these rules, and one draw needn't show every extreme that they name: For query head h and query block b, block_lists[h, b, :] names 8 different key blocks. Call the rows of b's index of ctx (a run of 128 rows) its shard c; every listed block lies on a key shard (a run of 1024 keys) at most 1 shards from c counted around the closed cycle of key shards in either direction, and at least one listed block lies exactly 1 shards away.
All inputs are finite; a program needn't handle non-finite values.
Results may differ from the reference program's by a relative error of at most 0.0065.
The reference program's roundings to bfloat16 on the way (of `key_scaled`, `value_scaled`, `rotated` and `weights_low`) count: a program that leaves them out, or rounds other values in their place, can miss the bound.
Values may be sent and summed in bfloat16 or wider, within the bound.
A program may use at most 64 MiB of HBM per device.

```python
import math
import jax
import jax.numpy as jnp
from jax import lax

DH = 128
GROUP = 16
BLOCK = 128
NSEL = 8
NSCALES = 16
ROW_DEV = 128
KEY_DEV = 1024
HEADS = 32
KV_HEADS = 2
ROWS = 512
KEYS = 4096
QBLOCKS = 4
KBLOCKS = 32
REACH = 1


def draw_queries(key, part):
    base_key = jax.random.fold_in(key, 0)
    drawn = jax.random.normal(base_key, (ROWS, HEADS, DH), jnp.float32)
    return jnp.clip(drawn, -16.0, 16.0).astype(jnp.bfloat16)


def draw_key_codes(key, part):
    base_key = jax.random.fold_in(key, 0)
    drawn = jax.random.normal(base_key, (KV_HEADS, KEYS, DH), jnp.float32)
    return jnp.clip(drawn, -16.0, 16.0).astype(jnp.bfloat16)


def draw_block_lists(key, part):
    blocks_dev = KEY_DEV // BLOCK
    cycle_size = KBLOCKS // blocks_dev
    window = (2 * REACH + 1) * blocks_dev
    rows_blocks = ROW_DEV // BLOCK
    first_key, second_key, third_key, fourth_key = jax.random.split(key, 4)
    shard_bias = jax.random.randint(first_key, (HEADS, cycle_size), 0, 4)
    random_part = jax.random.randint(second_key, (HEADS, QBLOCKS, window), 0, 16384)
    home_shard = jnp.arange(QBLOCKS, dtype=jnp.int32) // rows_blocks
    slot_ids = jnp.arange(window, dtype=jnp.int32)
    offsets = slot_ids // blocks_dev - REACH
    target_shard = jnp.mod(home_shard[:, None] + offsets[None, :], cycle_size)
    bias_table = shard_bias[:, target_shard]
    scores = (random_part + bias_table * 16384) * window + slot_ids[None, None, :]
    far_side = jax.random.randint(third_key, (HEADS, QBLOCKS), 0, 2)
    far_slot = jax.random.randint(fourth_key, (HEADS, QBLOCKS), 0, blocks_dev) + far_side * (window - blocks_dev)
    scores = jnp.where(slot_ids[None, None, :] == far_slot[:, :, None], 1 << 29, scores)
    top_values, chosen = lax.top_k(scores, NSEL)
    start_block = (home_shard - REACH) * blocks_dev
    return jnp.mod(start_block[None, :, None] + chosen, KBLOCKS).astype(jnp.int32)


def with_ends(values, own_key, smallest, high):
    dims = values.shape
    place = [jax.random.randint(jax.random.fold_in(own_key, axis), (), 0, dims[axis]) for axis in range(len(dims))]
    values = values.at[tuple(place)].set(smallest)
    longest = dims.index(max(dims))
    place[longest] = (place[longest] + 1) % dims[longest]
    return values.at[tuple(place)].set(high)


def block_levels(own_key, extent, pieces, low, largest):
    def one(position, parts):
        draws = jax.random.uniform(jax.random.fold_in(jax.random.fold_in(own_key, 6), position), (parts,), jnp.float32, low / len(pieces), largest / len(pieces))
        return jnp.repeat(jnp.exp(draws), extent[position] // parts).reshape((-1,) + (1,) * (len(extent) - position - 1))

    gain = one(*pieces[0])
    for cut in pieces[1:]:
        gain = gain * one(*cut)
    return gain


def gaussian(stream_key, dims, deviation, reach, shards=(), held_as=jnp.bfloat16):
    result = deviation * jax.random.normal(stream_key, dims, jnp.float32)
    if shards:
        result = result * block_levels(stream_key, dims, shards, -0.22, 0.18)
    return jnp.clip(result, -reach, reach).astype(held_as)


def setup_inputs(seed: int = 0, part: int = 0) -> dict:
    streams_of = jax.random.split(jax.random.key(seed), 8)
    part_keys = jax.random.split(jax.random.fold_in(streams_of[7], part), 8)
    queries = draw_queries(jax.random.fold_in(jax.random.fold_in(streams_of[7], part), 71), part)
    positions = with_ends(jax.random.randint(part_keys[1], (ROWS,), KEYS, KEYS + 4 * ROWS), jax.random.fold_in(part_keys[1], 1), KEYS, (KEYS + 4 * ROWS) - 1).astype(jnp.int32)
    key_codes = draw_key_codes(jax.random.fold_in(jax.random.fold_in(streams_of[7], part), 71), part)
    value_codes = gaussian(part_keys[3], (KV_HEADS, KEYS, DH), 1.0, 8.0, ((1, 4),))
    scale_index = with_ends(jax.random.randint(part_keys[4], (2, KV_HEADS, KBLOCKS), 0, NSCALES), jax.random.fold_in(part_keys[4], 1), 0, NSCALES - 1).astype(jnp.int32)
    scale_table = jnp.clip(jnp.exp(jax.random.uniform(streams_of[5], (2, NSCALES), jnp.float32, math.log(0.5), math.log(2.0))), 0.5, 2.0)
    block_lists = draw_block_lists(jax.random.fold_in(jax.random.fold_in(streams_of[7], part), 71), part)
    return {"queries": queries, "positions": positions, "key_codes": key_codes, "value_codes": value_codes, "scale_index": scale_index, "scale_table": scale_table, "block_lists": block_lists}


ROPE_BASE = 500000.0
FLOOR_VALUE = -1e+30

def rotate(queries, positions):
    halves = queries.shape[2] // 2
    frequency = ROPE_BASE ** (-2.0 * jnp.arange(halves, dtype=jnp.float32) / queries.shape[2])
    angles = positions.astype(jnp.float32)[:, None] * frequency[None, :]
    cosine = jnp.cos(angles)[:, None, :]
    sine_value = jnp.sin(angles)[:, None, :]
    paired = queries.astype(jnp.float32).reshape(queries.shape[0], queries.shape[1], halves, 2)
    even_part = paired[..., 0]
    odd_part = paired[..., 1]
    turned = jnp.stack([even_part * cosine - odd_part * sine_value, even_part * sine_value + odd_part * cosine], axis=-1)
    return turned.reshape(queries.shape).astype(jnp.bfloat16)

def dequantize(code_array, index_rows, table_row):
    scales = table_row[index_rows]
    blocks = code_array.astype(jnp.float32).reshape(code_array.shape[0], -1, BLOCK, code_array.shape[2]) * scales[:, :, None, None]
    return blocks.reshape(code_array.shape).astype(jnp.bfloat16)

def reference(queries, positions, key_codes, value_codes, scale_index, scale_table, block_lists):
    key_scaled = dequantize(key_codes, scale_index[0], scale_table[0])
    value_scaled = dequantize(value_codes, scale_index[1], scale_table[1])
    rotated = jnp.transpose(rotate(queries, positions), (1, 0, 2))
    cycle_size = KEYS // KEY_DEV
    key_ids = jnp.arange(KBLOCKS, dtype=jnp.int32)

    def attend_head(head_number):
        head_rows = rotated[head_number]
        shared = head_number // GROUP
        head_keys = key_scaled[shared]
        head_values = value_scaled[shared]
        head_lists = block_lists[head_number]
        block_mask = jnp.any(head_lists[:, :, None] == key_ids[None, None, :], axis=1)
        allowed = jnp.repeat(jnp.repeat(block_mask, BLOCK, axis=0), BLOCK, axis=1).reshape(ROWS, cycle_size, KEY_DEV)
        scores = jnp.dot(head_rows, head_keys.T, preferred_element_type=jnp.float32) / math.sqrt(DH)
        scores = scores.reshape(ROWS, cycle_size, KEY_DEV)
        shard_max = lax.optimization_barrier(jnp.max(jnp.where(allowed, scores, FLOOR_VALUE), axis=2))
        weights = jnp.where(allowed, jnp.exp(scores - shard_max[:, :, None]), 0.0)
        shard_sum = lax.optimization_barrier(jnp.sum(weights, axis=2))
        weights_low = weights.astype(jnp.bfloat16)
        shard_out = jnp.einsum('rsk,skd->rsd', weights_low.astype(jnp.float32), head_values.reshape(cycle_size, KEY_DEV, DH).astype(jnp.float32))
        total_max = lax.optimization_barrier(jnp.max(shard_max, axis=1))
        factor = jnp.exp(shard_max - total_max[:, None])
        total_sum = lax.optimization_barrier(jnp.sum(factor * shard_sum, axis=1))
        total_out = lax.optimization_barrier(jnp.sum(factor[:, :, None] * shard_out, axis=1))
        return (total_out / total_sum[:, None]).astype(jnp.bfloat16)
    per_head = lax.map(attend_head, jnp.arange(HEADS, dtype=jnp.int32))
    return jnp.transpose(per_head, (1, 0, 2)).reshape(ROWS, HEADS * DH)
```

```python
import functools
import math

import jax
import jax.numpy as jnp
import numpy as np
from jax import lax
from jax.experimental import pallas as pl
from jax.experimental.pallas import tpu as pltpu
from jax.sharding import PartitionSpec as P

GROUP = 16
BLOCK = 128
ROPE_BASE = 500000.0
PIECES = 1
CUTS = 1
MESH = pl.DeviceIdType.MESH


def attend(
    reach, n_ctx, n_head,
    lists_hbm, index_hbm, table_hbm, pos_hbm, freq_hbm, q_hbm, k_hbm, v_hbm,
    out_ref,
    lists_s, index_s, table_s, pos_ref, freq_ref,
    qcode, kcode, vcode, qwide, qrot, kbuf, vbuf, wbuf, lbuf, obuf,
    load_sem, ksend, krecv, vsend, vrecv, kfs, kfr, vfs, vfr, osend, orecv, own_sem,
):
    c = lax.axis_index("ctx")
    hp = lax.axis_index("head")
    heads, rows, dh = qrot.shape
    keys = kcode.shape[0]
    kblocks = keys // BLOCK
    nsel = lists_s.shape[2]
    rows_per = out_ref.shape[0]
    slots = 2 * reach + 1
    half = lax.rem(hp, 2)
    sib = hp + 1 - 2 * half
    kv_head = hp * heads // GROUP

    barrier = pltpu.get_barrier_semaphore()
    offsets = [o for d in range(1, reach + 1) for o in (d, -d)]
    for o in offsets:
        pl.semaphore_signal(
            barrier, inc=1, device_id={"ctx": lax.rem(c + o + n_ctx, n_ctx)}, device_id_type=MESH
        )
    for k in range(1, n_head):
        pl.semaphore_signal(
            barrier, inc=1, device_id={"head": lax.rem(hp + k, n_head)}, device_id_type=MESH
        )

    k_load = pltpu.make_async_copy(k_hbm.at[kv_head], kcode, load_sem.at[0])
    v_load = pltpu.make_async_copy(v_hbm.at[kv_head], vcode, load_sem.at[1])
    q_load = pltpu.make_async_copy(q_hbm, qcode, load_sem.at[2])
    small = [
        pltpu.make_async_copy(src, dst, load_sem.at[3 + i])
        for i, (src, dst) in enumerate(
            [
                (index_hbm, index_s),
                (table_hbm, table_s),
                (lists_hbm, lists_s),
                (pos_hbm, pos_ref),
                (freq_hbm, freq_ref),
            ]
        )
    ]
    k_load.start()
    for copy in small[:2]:
        copy.start()
    v_load.start()
    q_load.start()
    for copy in small[2:]:
        copy.start()

    own = reach * kblocks
    for copy in small[:2]:
        copy.wait()
    k_load.wait()
    for b in range(kblocks):
        s = table_s[0, index_s[0, kv_head, b]]
        kbuf[own + b] = (kcode[b * BLOCK : (b + 1) * BLOCK, :].astype(jnp.float32) * s).astype(
            jnp.bfloat16
        )

    part = kblocks // 2 // PIECES
    cuts = vsend.shape[1]
    wide = dh // cuts

    def k_copy(o, piece):
        return pltpu.make_async_remote_copy(
            src_ref=kbuf.at[pl.ds(own + half * (kblocks // 2) + piece * part, part)],
            dst_ref=kbuf.at[
                pl.ds((reach - o) * kblocks + half * (kblocks // 2) + piece * part, part)
            ],
            send_sem=ksend.at[reach - o, piece],
            recv_sem=krecv.at[reach - o, piece],
            device_id={"ctx": lax.rem(c + o + n_ctx, n_ctx)},
            device_id_type=MESH,
        )

    def v_copy(o, piece):
        return pltpu.make_async_remote_copy(
            src_ref=vbuf.at[pl.ds(own + half * (kblocks // 2), kblocks // 2), pl.ds(piece * wide, wide)],
            dst_ref=vbuf.at[
                pl.ds((reach - o) * kblocks + half * (kblocks // 2), kblocks // 2),
                pl.ds(piece * wide, wide),
            ],
            send_sem=vsend.at[reach - o, piece],
            recv_sem=vrecv.at[reach - o, piece],
            device_id={"ctx": lax.rem(c + o + n_ctx, n_ctx)},
            device_id_type=MESH,
        )

    def k_forward(slot, piece, which):
        region = kbuf.at[pl.ds(slot * kblocks + which * (kblocks // 2) + piece * part, part)]
        return forward(region, kfs, kfr, slot, piece)

    def v_forward(slot, piece, which):
        region = vbuf.at[
            pl.ds(slot * kblocks + which * (kblocks // 2), kblocks // 2), pl.ds(piece * wide, wide)
        ]
        return forward(region, vfs, vfr, slot, piece)

    def forward(region, send, recv, slot, piece):
        return pltpu.make_async_remote_copy(
            src_ref=region,
            dst_ref=region,
            send_sem=send.at[slot, piece],
            recv_sem=recv.at[slot, piece],
            device_id={"head": sib},
            device_id_type=MESH,
        )

    pl.semaphore_wait(barrier, len(offsets) + n_head - 1)
    for piece in range(PIECES):
        for o in offsets:
            k_copy(o, piece).start()

    v_load.wait()
    for b in range(kblocks):
        s = table_s[1, index_s[1, kv_head, b]]
        rounded = (vcode[b * BLOCK : (b + 1) * BLOCK, :].astype(jnp.float32) * s).astype(jnp.bfloat16)
        vbuf[own + b] = rounded.astype(jnp.float32).T.astype(jnp.bfloat16)
    for piece in range(cuts):
        for o in offsets:
            v_copy(o, piece).start()

    q_load.wait()
    for copy in small[2:]:
        copy.wait()
    qwide[...] = qcode[...].astype(jnp.float32)
    pos = jnp.broadcast_to(pos_ref[...].astype(jnp.float32), (rows, rows)).T
    angle = pos * freq_ref[...]
    lane = lax.broadcasted_iota(jnp.int32, (rows, dh), 1)
    even = lax.rem(lane, 2) == 0
    cosine = jnp.cos(angle)
    sine = jnp.sin(angle)
    sine = jnp.where(even, -sine, sine)
    for h in range(heads):
        x = qwide[pl.ds(h, rows, stride=heads), :]
        other = jnp.where(even, pltpu.roll(x, dh - 1, 1), pltpu.roll(x, 1, 1))
        qrot[h] = (x * cosine + other * sine).astype(jnp.bfloat16)

    for piece in range(PIECES):
        for o in offsets:
            k_copy(o, piece).wait_recv()
            k_forward(reach - o, piece, half).start()
    for piece in range(PIECES):
        for o in offsets:
            k_forward(reach - o, piece, 1 - half).wait_recv()

    total = n_ctx * kblocks
    base = total - (c - reach) * kblocks
    factor = math.log2(math.e) / math.sqrt(dh)

    def block_of(h, j):
        return jnp.minimum(lax.rem(lists_s[h, c, j] + base, total), slots * kblocks - 1)

    def score(h, carry):
        gathered = jnp.concatenate([kbuf[block_of(h, j)] for j in range(nsel)], axis=0)
        s = lax.dot_general(
            gathered, qrot[h], (((1,), (1,)), ((), ())), preferred_element_type=jnp.float32
        )
        m = jnp.max(s, axis=0, keepdims=True)
        w = jnp.exp2((s - m) * factor)
        lbuf[h] = 1.0 / jnp.sum(w, axis=0, keepdims=True)
        wbuf[h] = w.astype(jnp.bfloat16)
        return carry

    lax.fori_loop(0, heads, score, 0, unroll=True)

    def columns(h):
        return pl.ds(pl.multiple_of((hp * heads + h) * dh, dh), dh)

    def o_copy(h, k):
        peer = lax.rem(hp + k, n_head)
        return pltpu.make_async_remote_copy(
            src_ref=obuf.at[h, peer],
            dst_ref=out_ref.at[:, columns(h)],
            send_sem=osend.at[h, k - 1],
            recv_sem=orecv.at[h, k - 1],
            device_id={"head": peer},
            device_id_type=MESH,
        )

    def own_copy(h):
        return pltpu.make_async_copy(obuf.at[h, hp], out_ref.at[:, columns(h)], own_sem.at[h])

    def value(h, carry):
        gathered = jnp.concatenate([vbuf[block_of(h, j)] for j in range(nsel)], axis=1)
        o = jnp.dot(gathered, wbuf[h], preferred_element_type=jnp.float32)
        t = (o * lbuf[h]).T
        for p in range(n_head):
            obuf[h, p] = t[p * rows_per : (p + 1) * rows_per, :].astype(jnp.bfloat16)
        for k in range(1, n_head):
            o_copy(h, k).start()
        own_copy(h).start()
        return carry

    for piece in range(cuts):
        for o in offsets:
            v_copy(o, piece).wait_recv()
            v_forward(reach - o, piece, half).start()
    for piece in range(cuts):
        for o in offsets:
            v_forward(reach - o, piece, 1 - half).wait_recv()
    lax.fori_loop(0, heads, value, 0, unroll=True)

    for o in offsets:
        for piece in range(PIECES):
            k_copy(o, piece).wait_send()
            k_forward(reach - o, piece, half).wait_send()
        for piece in range(cuts):
            v_copy(o, piece).wait_send()
            v_forward(reach - o, piece, half).wait_send()

    def finish(h, carry):
        own_copy(h).wait()
        for k in range(1, n_head):
            o_copy(h, k).wait()
        return carry

    lax.fori_loop(0, heads, finish, 0)


def on_device(queries, positions, key_codes, value_codes, scale_index, scale_table, block_lists):
    n_ctx = lax.axis_size("ctx")
    n_head = lax.axis_size("head")
    reach = min(3, (n_ctx - 1) // 2)
    rows, heads, dh = queries.shape
    keys = key_codes.shape[1]
    kblocks = keys // BLOCK
    nsel = block_lists.shape[2]
    slots = 2 * reach + 1
    assert rows == BLOCK and n_head % 2 == 0 and GROUP % (2 * heads) == 0
    exponents = -2.0 * np.repeat(np.arange(dh // 2), 2) / dh
    freq = jnp.asarray((ROPE_BASE**exponents).astype(np.float32)[None, :])
    bf16, f32 = jnp.bfloat16, jnp.float32
    dma = pltpu.SemaphoreType.DMA
    hbm = pl.BlockSpec(memory_space=pltpu.HBM)
    return pl.pallas_call(
        functools.partial(attend, reach, n_ctx, n_head),
        out_shape=pltpu.VMEM((rows // n_head, n_head * heads * dh), bf16),
        in_specs=[hbm] * 8,
        out_specs=pl.BlockSpec(memory_space=pltpu.VMEM),
        scratch_shapes=[
            pltpu.SMEM(block_lists.shape, jnp.int32),
            pltpu.SMEM(scale_index.shape, jnp.int32),
            pltpu.SMEM(scale_table.shape, f32),
            pltpu.VMEM((1, rows), jnp.int32),
            pltpu.VMEM((1, dh), f32),
            pltpu.VMEM((rows * heads, dh), bf16),
            pltpu.VMEM((keys, dh), bf16),
            pltpu.VMEM((keys, dh), bf16),
            pltpu.VMEM((rows * heads, dh), f32),
            pltpu.VMEM((heads, rows, dh), bf16),
            pltpu.VMEM((slots * kblocks, BLOCK, dh), bf16),
            pltpu.VMEM((slots * kblocks, dh, BLOCK), bf16),
            pltpu.VMEM((heads, nsel * BLOCK, rows), bf16),
            pltpu.VMEM((heads, 1, rows), f32),
            pltpu.VMEM((heads, n_head, rows // n_head, dh), bf16),
            dma((8,)),
            dma((slots, PIECES)),
            dma((slots, PIECES)),
            dma((slots, CUTS)),
            dma((slots, CUTS)),
            dma((slots, PIECES)),
            dma((slots, PIECES)),
            dma((slots, CUTS)),
            dma((slots, CUTS)),
            dma((heads, n_head - 1)),
            dma((heads, n_head - 1)),
            dma((heads,)),
        ],
        compiler_params=pltpu.CompilerParams(
            collective_id=0, has_side_effects=True, vmem_limit_bytes=67043328 - 2 * rows * heads * dh
        ),
        name="attend",
    )(
        block_lists,
        scale_index,
        scale_table,
        positions.reshape(1, rows),
        freq,
        queries.reshape(rows * heads, dh),
        key_codes,
        value_codes,
    )


def solution(mesh):
    placed = (
        P(("groups", "ctx"), "head", None),
        P(("groups", "ctx")),
        P("groups", "ctx", None),
        P("groups", "ctx", None),
        P("groups", None, "ctx"),
        P(),
        P(("groups", "head"), None, None),
    )
    return jax.shard_map(
        on_device,
        mesh=mesh,
        in_specs=placed,
        out_specs=P(("groups", "ctx", "head"), None),
        check_vma=False,
    )
```

```python
import functools
import math

import jax
import jax.numpy as jnp
import numpy as np
from jax import lax
from jax.experimental import pallas as pl
from jax.experimental.pallas import tpu as pltpu
from jax.sharding import PartitionSpec as P

GROUP = 16
BLOCK = 128
ROPE_BASE = 500000.0
CUTS = (2, 2)
BUNCHES = 1
MESH = pl.DeviceIdType.MESH


def attend(
    reach, n_ctx, n_head,
    lists_hbm, index_hbm, table_hbm, pos_hbm, freq_hbm, q_hbm, k_hbm, v_hbm,
    out_ref,
    lists_s, index_s, table_s, pos_ref, freq_ref,
    qcode, kcode, vcode, qwide, qrot, kbuf, vbuf, wbuf, lbuf, obuf, stage,
    load_sem, isend, irecv, ksend, krecv, vsend, vrecv, kfs, kfr, vfs, vfr, osend, orecv,
    ctx_in, head_in,
):
    c = lax.axis_index("ctx")
    hp = lax.axis_index("head")
    heads, rows, dh = qrot.shape
    kblocks = kcode.shape[1]
    nsel = lists_s.shape[2]
    rows_per = out_ref.shape[0]
    slots = 2 * reach + 1
    half = lax.rem(hp, 2)
    sib = hp + 1 - 2 * half
    kv_head = hp * heads // GROUP

    offsets = [o for d in range(1, reach + 1) for o in (d, -d)]
    others = range(1, n_head)

    def ctx_of(o):
        return lax.rem(c + o + n_ctx, n_ctx)

    def head_of(k):
        return lax.rem(hp + k, n_head)

    def rank(h):
        return h + 1 - 2 * lax.rem(h, 2)

    barrier = pltpu.get_barrier_semaphore()
    greeted = rank(hp)
    for o in offsets:
        greeted += (ctx_of(o) < c).astype(jnp.int32)

        @pl.when(ctx_of(o) > c)
        def _():
            pl.semaphore_signal(barrier, inc=1, device_id={"ctx": ctx_of(o)}, device_id_type=MESH)

    for k in others:

        @pl.when(rank(head_of(k)) > rank(hp))
        def _():
            pl.semaphore_signal(barrier, inc=1, device_id={"head": head_of(k)}, device_id_type=MESH)

    k_load = pltpu.make_async_copy(k_hbm.at[kv_head], kcode.at[reach], load_sem.at[0])
    v_load = pltpu.make_async_copy(v_hbm.at[kv_head], vcode, load_sem.at[1])
    q_load = pltpu.make_async_copy(q_hbm, qcode, load_sem.at[2])
    small = [
        pltpu.make_async_copy(src, dst, load_sem.at[3 + i])
        for i, (src, dst) in enumerate(
            [
                (index_hbm, index_s.at[reach]),
                (table_hbm, table_s),
                (lists_hbm, lists_s),
                (pos_hbm, pos_ref),
                (freq_hbm, freq_ref),
            ]
        )
    ]
    v_load.start()
    for copy in small:
        copy.start()
    k_load.start()
    q_load.start()

    own = reach * kblocks
    part = kblocks // 2
    cuts = len(vbuf)
    wides = [ref.shape[1] for ref in vbuf]
    firsts = [sum(wides[:piece]) for piece in range(cuts)]

    def i_copy(o):
        return pltpu.make_async_remote_copy(
            src_ref=index_hbm,
            dst_ref=index_s.at[reach - o],
            send_sem=isend.at[reach - o],
            recv_sem=irecv.at[reach - o],
            device_id={"ctx": ctx_of(o)},
            device_id_type=MESH,
        )

    def k_copy(o):
        return pltpu.make_async_remote_copy(
            src_ref=k_hbm.at[kv_head, pl.ds(half * part, part)],
            dst_ref=kcode.at[reach - o, pl.ds(half * part, part)],
            send_sem=ksend.at[reach - o],
            recv_sem=krecv.at[reach - o],
            device_id={"ctx": ctx_of(o)},
            device_id_type=MESH,
        )

    def v_copy(o, piece):
        return pltpu.make_async_remote_copy(
            src_ref=vbuf[piece].at[pl.ds(own + half * part, part)],
            dst_ref=vbuf[piece].at[
                pl.ds((reach - o) * kblocks + half * part, part)
            ],
            send_sem=vsend.at[reach - o, piece],
            recv_sem=vrecv.at[reach - o, piece],
            device_id={"ctx": ctx_of(o)},
            device_id_type=MESH,
        )

    def k_forward(slot, which):
        region = kcode.at[slot, pl.ds(which * part, part)]
        return forward(region, kfs.at[slot], kfr.at[slot])

    def v_forward(slot, piece, which):
        region = vbuf[piece].at[pl.ds(slot * kblocks + which * (part), part)]
        return forward(region, vfs.at[slot, piece], vfr.at[slot, piece])

    def forward(region, send, recv):
        return pltpu.make_async_remote_copy(
            src_ref=region,
            dst_ref=region,
            send_sem=send,
            recv_sem=recv,
            device_id={"head": sib},
            device_id_type=MESH,
        )

    def start_keys(o):
        k_copy(o).start()
        i_copy(o).start()

    def start_values(o):
        for piece in range(cuts):
            v_copy(o, piece).start()

    def on_core(which, order, lower, step):
        for o in order:
            side = ctx_of(o) < c if lower else ctx_of(o) > c
            pl.when(jnp.logical_and(half == which, side))(functools.partial(step, o))

    @pl.when(greeted > 0)
    def _():
        pl.semaphore_wait(barrier, greeted)

    on_core(0, offsets, True, start_keys)
    on_core(1, offsets, True, start_keys)
    for o in offsets:

        @pl.when(ctx_of(o) < c)
        def _():
            pl.semaphore_signal(
                ctx_in.at[reach - o], inc=1, device_id={"ctx": ctx_of(o)}, device_id_type=MESH
            )

    for k in others:

        @pl.when(rank(head_of(k)) < rank(hp))
        def _():
            pl.semaphore_signal(
                head_in.at[n_head - k - 1], inc=1, device_id={"head": head_of(k)}, device_id_type=MESH
            )

    def greet_head(k):
        @pl.when(rank(head_of(k)) > rank(hp))
        def _():
            pl.semaphore_wait(head_in.at[k - 1], 1)

    def scale_key(slot, b):
        s = table_s[0, index_s[slot, 0, kv_head, b]]
        kbuf[slot * kblocks + b] = (kcode[slot, b].astype(jnp.float32) * s).astype(jnp.bfloat16)

    v_load.wait()
    for copy in small[:2]:
        copy.wait()
    for b in range(kblocks):
        s = table_s[1, index_s[reach, 1, kv_head, b]]
        rounded = (vcode[b * BLOCK : (b + 1) * BLOCK, :].astype(jnp.float32) * s).astype(jnp.bfloat16)
        turned = rounded.astype(jnp.float32).T
        for piece in range(cuts):
            first, wide = firsts[piece], wides[piece]
            vbuf[piece][own + b] = turned[first : first + wide, :].astype(jnp.bfloat16)
    on_core(0, offsets, True, start_values)
    on_core(1, offsets, True, start_values)

    k_load.wait()
    for b in range(kblocks):
        scale_key(reach, b)

    def greet_keys(o):
        pl.semaphore_wait(ctx_in.at[reach + o], 1)
        start_keys(o)

    def greet_both(o):
        greet_keys(o)
        start_values(o)

    on_core(0, offsets, False, greet_both)
    on_core(1, offsets, False, greet_keys)
    on_core(1, offsets[::-1], False, start_values)

    q_load.wait()
    for copy in small[2:]:
        copy.wait()
    qwide[...] = qcode[...].astype(jnp.float32)
    pos = jnp.broadcast_to(pos_ref[...].astype(jnp.float32), (rows, rows)).T
    angle = pos * freq_ref[...]
    lane = lax.broadcasted_iota(jnp.int32, (rows, dh), 1)
    even = lax.rem(lane, 2) == 0
    cosine = jnp.cos(angle)
    sine = jnp.sin(angle)
    sine = jnp.where(even, -sine, sine)
    for h in range(heads):
        x = qwide[pl.ds(h, rows, stride=heads), :]
        other = jnp.where(even, pltpu.roll(x, dh - 1, 1), pltpu.roll(x, 1, 1))
        qrot[h] = (x * cosine + other * sine).astype(jnp.bfloat16)

    for k in others:
        greet_head(k)
    for o in offsets:
        k_copy(o).wait_recv()
        k_forward(reach - o, half).start()
        i_copy(o).wait_recv()
        for b in range(part):
            scale_key(reach - o, half * part + b)
    for o in offsets:
        k_forward(reach - o, 1 - half).wait_recv()
        for b in range(part):
            scale_key(reach - o, (1 - half) * part + b)

    total = n_ctx * kblocks
    base = total - (c - reach) * kblocks
    factor = math.log2(math.e) / math.sqrt(dh)

    def block_of(h, j):
        return jnp.minimum(lax.rem(lists_s[h, c, j] + base, total), slots * kblocks - 1)

    def score(h, carry):
        gathered = jnp.concatenate([kbuf[block_of(h, j)] for j in range(nsel)], axis=0)
        s = lax.dot_general(
            gathered, qrot[h], (((1,), (1,)), ((), ())), preferred_element_type=jnp.float32
        )
        m = jnp.max(s, axis=0, keepdims=True)
        w = jnp.exp2((s - m) * factor)
        lbuf[h] = 1.0 / jnp.sum(w, axis=0, keepdims=True)
        wbuf[h] = w.astype(jnp.bfloat16)
        return carry

    lax.fori_loop(0, heads, score, 0, unroll=True)

    def o_copy(piece, bunch, k):
        peer = head_of(k)
        size = obuf[piece].shape[1] // BUNCHES
        region = pl.ds(bunch * size, size)
        return pltpu.make_async_remote_copy(
            src_ref=obuf[piece].at[peer, region],
            dst_ref=stage[piece].at[hp, region],
            send_sem=osend.at[piece, bunch, k - 1],
            recv_sem=orecv.at[piece, bunch, k - 1],
            device_id={"head": peer},
            device_id_type=MESH,
        )

    def value(piece, g):
        pack = dh // wides[piece]
        parts = []
        for h in range(g * pack, (g + 1) * pack):
            gathered = jnp.concatenate([vbuf[piece][block_of(h, j)] for j in range(nsel)], axis=1)
            o = jnp.dot(gathered, wbuf[h], preferred_element_type=jnp.float32)
            parts.append(o * lbuf[h])
        t = jnp.concatenate(parts, axis=0).T
        for p in range(n_head):
            obuf[piece][p, g] = t[p * rows_per : (p + 1) * rows_per, :].astype(jnp.bfloat16)

    out_lane = lax.broadcasted_iota(jnp.int32, (rows_per, dh), 1)

    def place(piece, source, ref):
        first, wide = firsts[piece], wides[piece]
        pack = dh // wide
        ours = jnp.logical_and(out_lane >= first, out_lane < first + wide)
        for g in range(ref.shape[0]):
            tile = ref[g].astype(jnp.float32)
            for i in range(pack):
                where = pl.ds(pl.multiple_of((source * heads + g * pack + i) * dh, dh), dh)
                shift = (first - i * wide) % dh
                moved = pltpu.roll(tile, shift, 1) if shift else tile
                if piece:
                    moved = jnp.where(ours, moved, out_ref[:, where].astype(jnp.float32))
                out_ref[:, where] = moved.astype(jnp.bfloat16)

    def pass_on(piece):
        for o in offsets:
            v_copy(o, piece).wait_recv()
            v_forward(reach - o, piece, half).start()

    pass_on(0)
    for piece in range(cuts):
        if piece + 1 < cuts:
            pass_on(piece + 1)
        for o in offsets:
            v_forward(reach - o, piece, 1 - half).wait_recv()
        groups = obuf[piece].shape[1]
        for bunch in range(BUNCHES):
            for g in range(groups // BUNCHES * bunch, groups // BUNCHES * (bunch + 1)):
                value(piece, g)
            for k in others:
                o_copy(piece, bunch, k).start()

    for piece in range(cuts):
        place(piece, hp, obuf[piece].at[hp])

    for o in offsets:
        i_copy(o).wait_send()
        k_copy(o).wait_send()
        k_forward(reach - o, half).wait_send()
        for piece in range(cuts):
            v_copy(o, piece).wait_send()
            v_forward(reach - o, piece, half).wait_send()

    for piece in range(cuts):
        for k in range(1, n_head):
            source = lax.rem(hp - k + n_head, n_head)
            for bunch in range(BUNCHES):
                o_copy(piece, bunch, k).wait_recv()
            place(piece, source, stage[piece].at[source])
    for piece in range(cuts):
        for k in range(1, n_head):
            for bunch in range(BUNCHES):
                o_copy(piece, bunch, k).wait_send()


def on_device(queries, positions, key_codes, value_codes, scale_index, scale_table, block_lists):
    n_ctx = lax.axis_size("ctx")
    n_head = lax.axis_size("head")
    reach = min(3, (n_ctx - 1) // 2)
    rows, heads, dh = queries.shape
    keys = key_codes.shape[1]
    kblocks = keys // BLOCK
    coded = key_codes.reshape(key_codes.shape[0], kblocks, BLOCK, dh)
    nsel = block_lists.shape[2]
    slots = 2 * reach + 1
    assert rows == BLOCK and n_head % 2 == 0 and GROUP % (2 * heads) == 0
    exponents = -2.0 * np.repeat(np.arange(dh // 2), 2) / dh
    freq = jnp.asarray((ROPE_BASE**exponents).astype(np.float32)[None, :])
    bf16, f32 = jnp.bfloat16, jnp.float32
    dma = pltpu.SemaphoreType.DMA
    hbm = pl.BlockSpec(memory_space=pltpu.HBM)
    return pl.pallas_call(
        functools.partial(attend, reach, n_ctx, n_head),
        out_shape=pltpu.VMEM((rows // n_head, n_head * heads * dh), bf16),
        in_specs=[hbm] * 8,
        out_specs=pl.BlockSpec(memory_space=pltpu.VMEM),
        scratch_shapes=[
            pltpu.SMEM(block_lists.shape, jnp.int32),
            pltpu.SMEM((slots,) + scale_index.shape, jnp.int32),
            pltpu.SMEM(scale_table.shape, f32),
            pltpu.VMEM((1, rows), jnp.int32),
            pltpu.VMEM((1, dh), f32),
            pltpu.VMEM((rows * heads, dh), bf16),
            pltpu.VMEM((slots, kblocks, BLOCK, dh), bf16),
            pltpu.VMEM((keys, dh), bf16),
            pltpu.VMEM((rows * heads, dh), f32),
            pltpu.VMEM((heads, rows, dh), bf16),
            pltpu.VMEM((slots * kblocks, BLOCK, dh), bf16),
            [pltpu.VMEM((slots * kblocks, dh // cut, BLOCK), bf16) for cut in CUTS],
            pltpu.VMEM((heads, nsel * BLOCK, rows), bf16),
            pltpu.VMEM((heads, 1, rows), f32),
            [pltpu.VMEM((n_head, heads // cut, rows // n_head, dh), bf16) for cut in CUTS],
            [pltpu.VMEM((n_head, heads // cut, rows // n_head, dh), bf16) for cut in CUTS],
            dma((8,)),
            dma((slots,)),
            dma((slots,)),
            dma((slots,)),
            dma((slots,)),
            dma((slots, len(CUTS))),
            dma((slots, len(CUTS))),
            dma((slots,)),
            dma((slots,)),
            dma((slots, len(CUTS))),
            dma((slots, len(CUTS))),
            dma((len(CUTS), BUNCHES, n_head - 1)),
            dma((len(CUTS), BUNCHES, n_head - 1)),
            pltpu.SemaphoreType.REGULAR((slots,)),
            pltpu.SemaphoreType.REGULAR((n_head - 1,)),
        ],
        compiler_params=pltpu.CompilerParams(
            collective_id=0, has_side_effects=True, vmem_limit_bytes=67043328 - 2 * rows * heads * dh
        ),
        name="attend",
    )(
        block_lists,
        scale_index,
        scale_table,
        positions.reshape(1, rows),
        freq,
        queries.reshape(rows * heads, dh),
        coded,
        value_codes,
    )


def solution(mesh):
    placed = (
        P(("groups", "ctx"), "head", None),
        P(("groups", "ctx")),
        P("groups", "ctx", None),
        P("groups", "ctx", None),
        P("groups", None, "ctx"),
        P(),
        P(("groups", "head"), None, None),
    )
    return jax.shard_map(
        on_device,
        mesh=mesh,
        in_specs=placed,
        out_specs=P(("groups", "ctx", "head"), None),
        check_vma=False,
    )
```

```python
import functools
import math

import jax
import jax.numpy as jnp
import numpy as np
from jax import lax
from jax.experimental import pallas as pl
from jax.experimental.pallas import tpu as pltpu
from jax.sharding import PartitionSpec as P

GROUP = 16
BLOCK = 128
ROPE_BASE = 500000.0
CUTS = (2, 2)
BUNCHES = 1
MESH = pl.DeviceIdType.MESH


def attend(
    reach, n_ctx, n_head,
    lists_hbm, index_hbm, table_hbm, pos_hbm, freq_hbm, q_hbm, k_hbm, v_hbm,
    out_ref,
    lists_s, index_s, table_s, pos_ref, freq_ref,
    qcode, kcode, vcode, qwide, qrot, kbuf, vbuf, wbuf, lbuf, obuf, stage,
    load_sem, isend, irecv, ksend, krecv, vsend, vrecv, kfs, kfr, vfs, vfr, osend, orecv,
    ctx_in, head_in,
):
    c = lax.axis_index("ctx")
    hp = lax.axis_index("head")
    heads, rows, dh = qrot.shape
    kblocks = kcode.shape[1]
    nsel = lists_s.shape[2]
    rows_per = out_ref.shape[0]
    slots = 2 * reach + 1
    half = lax.rem(hp, 2)
    sib = hp + 1 - 2 * half
    kv_head = hp * heads // GROUP

    offsets = [o for d in range(1, reach + 1) for o in (d, -d)]
    others = range(1, n_head)

    def ctx_of(o):
        return lax.rem(c + o + n_ctx, n_ctx)

    def head_of(k):
        return lax.rem(hp + k, n_head)

    def rank(h):
        return n_head - 1 - h

    barrier = pltpu.get_barrier_semaphore()
    greeted = rank(hp)
    for o in offsets:
        greeted += (ctx_of(o) < c).astype(jnp.int32)

        @pl.when(ctx_of(o) > c)
        def _():
            pl.semaphore_signal(barrier, inc=1, device_id={"ctx": ctx_of(o)}, device_id_type=MESH)

    for k in others:

        @pl.when(rank(head_of(k)) > rank(hp))
        def _():
            pl.semaphore_signal(barrier, inc=1, device_id={"head": head_of(k)}, device_id_type=MESH)

    k_load = pltpu.make_async_copy(k_hbm.at[kv_head], kcode.at[reach], load_sem.at[0])
    v_load = pltpu.make_async_copy(v_hbm.at[kv_head], vcode, load_sem.at[1])
    q_load = pltpu.make_async_copy(q_hbm, qcode, load_sem.at[2])
    small = [
        pltpu.make_async_copy(src, dst, load_sem.at[3 + i])
        for i, (src, dst) in enumerate(
            [
                (index_hbm, index_s.at[reach]),
                (table_hbm, table_s),
                (lists_hbm, lists_s),
                (pos_hbm, pos_ref),
                (freq_hbm, freq_ref),
            ]
        )
    ]
    v_load.start()
    for copy in small:
        copy.start()
    k_load.start()
    q_load.start()

    own = reach * kblocks
    part = kblocks // 2
    cuts = len(vbuf)
    wides = [ref.shape[1] for ref in vbuf]
    firsts = [sum(wides[:piece]) for piece in range(cuts)]

    def i_copy(o):
        return pltpu.make_async_remote_copy(
            src_ref=index_hbm,
            dst_ref=index_s.at[reach - o],
            send_sem=isend.at[reach - o],
            recv_sem=irecv.at[reach - o],
            device_id={"ctx": ctx_of(o)},
            device_id_type=MESH,
        )

    def k_copy(o):
        return pltpu.make_async_remote_copy(
            src_ref=k_hbm.at[kv_head, pl.ds(half * part, part)],
            dst_ref=kcode.at[reach - o, pl.ds(half * part, part)],
            send_sem=ksend.at[reach - o],
            recv_sem=krecv.at[reach - o],
            device_id={"ctx": ctx_of(o)},
            device_id_type=MESH,
        )

    def v_copy(o, piece):
        return pltpu.make_async_remote_copy(
            src_ref=vbuf[piece].at[pl.ds(own + half * part, part)],
            dst_ref=vbuf[piece].at[
                pl.ds((reach - o) * kblocks + half * part, part)
            ],
            send_sem=vsend.at[reach - o, piece],
            recv_sem=vrecv.at[reach - o, piece],
            device_id={"ctx": ctx_of(o)},
            device_id_type=MESH,
        )

    def k_forward(slot, which):
        region = kcode.at[slot, pl.ds(which * part, part)]
        return forward(region, kfs.at[slot], kfr.at[slot])

    def v_forward(slot, piece, which):
        region = vbuf[piece].at[pl.ds(slot * kblocks + which * (part), part)]
        return forward(region, vfs.at[slot, piece], vfr.at[slot, piece])

    def forward(region, send, recv):
        return pltpu.make_async_remote_copy(
            src_ref=region,
            dst_ref=region,
            send_sem=send,
            recv_sem=recv,
            device_id={"head": sib},
            device_id_type=MESH,
        )

    def start_keys(o):
        k_copy(o).start()
        i_copy(o).start()

    def start_values(o):
        for piece in range(cuts):
            v_copy(o, piece).start()

    def start_value(piece, o):
        v_copy(o, piece).start()

    def on_core(which, order, lower, step):
        for o in order:
            side = ctx_of(o) < c if lower else ctx_of(o) > c
            pl.when(jnp.logical_and(half == which, side))(functools.partial(step, o))

    @pl.when(greeted > 0)
    def _():
        pl.semaphore_wait(barrier, greeted)

    on_core(0, offsets, True, start_keys)
    on_core(1, offsets, True, start_keys)
    for o in offsets:

        @pl.when(ctx_of(o) < c)
        def _():
            pl.semaphore_signal(
                ctx_in.at[reach - o], inc=1, device_id={"ctx": ctx_of(o)}, device_id_type=MESH
            )

    for k in others:

        @pl.when(rank(head_of(k)) < rank(hp))
        def _():
            pl.semaphore_signal(
                head_in.at[n_head - k - 1], inc=1, device_id={"head": head_of(k)}, device_id_type=MESH
            )

    def greet_head(k):
        @pl.when(rank(head_of(k)) > rank(hp))
        def _():
            pl.semaphore_wait(head_in.at[k - 1], 1)

    def scale_key(slot, b):
        s = table_s[0, index_s[slot, 0, kv_head, b]]
        kbuf[slot * kblocks + b] = (kcode[slot, b].astype(jnp.float32) * s).astype(jnp.bfloat16)

    v_load.wait()
    for copy in small[:2]:
        copy.wait()
    for b in range(kblocks):
        s = table_s[1, index_s[reach, 1, kv_head, b]]
        rounded = (vcode[b * BLOCK : (b + 1) * BLOCK, :].astype(jnp.float32) * s).astype(jnp.bfloat16)
        turned = rounded.astype(jnp.float32).T
        for piece in range(cuts):
            first, wide = firsts[piece], wides[piece]
            vbuf[piece][own + b] = turned[first : first + wide, :].astype(jnp.bfloat16)
    on_core(0, offsets, True, start_values)
    on_core(1, offsets, True, start_values)

    k_load.wait()
    for b in range(kblocks):
        scale_key(reach, b)

    def greet_keys(o):
        pl.semaphore_wait(ctx_in.at[reach + o], 1)
        start_keys(o)

    def greet_both(o):
        greet_keys(o)
        start_values(o)

    on_core(0, offsets, False, greet_keys)
    on_core(1, offsets, False, greet_keys)
    for piece in range(cuts):
        on_core(0, offsets, False, functools.partial(start_value, piece))
        on_core(1, offsets, False, functools.partial(start_value, piece))

    q_load.wait()
    for copy in small[2:]:
        copy.wait()
    qwide[...] = qcode[...].astype(jnp.float32)
    pos = jnp.broadcast_to(pos_ref[...].astype(jnp.float32), (rows, rows)).T
    angle = pos * freq_ref[...]
    lane = lax.broadcasted_iota(jnp.int32, (rows, dh), 1)
    even = lax.rem(lane, 2) == 0
    cosine = jnp.cos(angle)
    sine = jnp.sin(angle)
    sine = jnp.where(even, -sine, sine)
    for h in range(heads):
        x = qwide[pl.ds(h, rows, stride=heads), :]
        other = jnp.where(even, pltpu.roll(x, dh - 1, 1), pltpu.roll(x, 1, 1))
        qrot[h] = (x * cosine + other * sine).astype(jnp.bfloat16)

    for k in others:
        greet_head(k)
    for o in offsets:
        k_copy(o).wait_recv()
        k_forward(reach - o, half).start()
        i_copy(o).wait_recv()
        for b in range(part):
            scale_key(reach - o, half * part + b)
    for o in offsets:
        k_forward(reach - o, 1 - half).wait_recv()
        for b in range(part):
            scale_key(reach - o, (1 - half) * part + b)

    total = n_ctx * kblocks
    base = total - (c - reach) * kblocks
    factor = math.log2(math.e) / math.sqrt(dh)

    def block_of(h, j):
        return jnp.minimum(lax.rem(lists_s[h, c, j] + base, total), slots * kblocks - 1)

    def score(h, carry):
        gathered = jnp.concatenate([kbuf[block_of(h, j)] for j in range(nsel)], axis=0)
        s = lax.dot_general(
            gathered, qrot[h], (((1,), (1,)), ((), ())), preferred_element_type=jnp.float32
        )
        m = jnp.max(s, axis=0, keepdims=True)
        w = jnp.exp2((s - m) * factor)
        lbuf[h] = 1.0 / jnp.sum(w, axis=0, keepdims=True)
        wbuf[h] = w.astype(jnp.bfloat16)
        return carry

    lax.fori_loop(0, heads, score, 0, unroll=True)

    def o_copy(piece, bunch, k):
        peer = head_of(k)
        size = obuf[piece].shape[1] // BUNCHES
        region = pl.ds(bunch * size, size)
        return pltpu.make_async_remote_copy(
            src_ref=obuf[piece].at[peer, region],
            dst_ref=stage[piece].at[hp, region],
            send_sem=osend.at[piece, bunch, k - 1],
            recv_sem=orecv.at[piece, bunch, k - 1],
            device_id={"head": peer},
            device_id_type=MESH,
        )

    def value(piece, g):
        pack = dh // wides[piece]
        parts = []
        for h in range(g * pack, (g + 1) * pack):
            gathered = jnp.concatenate([vbuf[piece][block_of(h, j)] for j in range(nsel)], axis=1)
            o = jnp.dot(gathered, wbuf[h], preferred_element_type=jnp.float32)
            parts.append(o * lbuf[h])
        t = jnp.concatenate(parts, axis=0).T
        for p in range(n_head):
            obuf[piece][p, g] = t[p * rows_per : (p + 1) * rows_per, :].astype(jnp.bfloat16)

    out_lane = lax.broadcasted_iota(jnp.int32, (rows_per, dh), 1)

    def place(piece, source, ref):
        first, wide = firsts[piece], wides[piece]
        pack = dh // wide
        ours = jnp.logical_and(out_lane >= first, out_lane < first + wide)
        for g in range(ref.shape[0]):
            tile = ref[g].astype(jnp.float32)
            for i in range(pack):
                where = pl.ds(pl.multiple_of((source * heads + g * pack + i) * dh, dh), dh)
                shift = (first - i * wide) % dh
                moved = pltpu.roll(tile, shift, 1) if shift else tile
                if piece:
                    moved = jnp.where(ours, moved, out_ref[:, where].astype(jnp.float32))
                out_ref[:, where] = moved.astype(jnp.bfloat16)

    def pass_on(piece):
        for o in offsets:
            v_copy(o, piece).wait_recv()
            v_forward(reach - o, piece, half).start()

    pass_on(0)
    for piece in range(cuts):
        if piece + 1 < cuts:
            pass_on(piece + 1)
        for o in offsets:
            v_forward(reach - o, piece, 1 - half).wait_recv()
        groups = obuf[piece].shape[1]
        for bunch in range(BUNCHES):
            for g in range(groups // BUNCHES * bunch, groups // BUNCHES * (bunch + 1)):
                value(piece, g)
            for k in others:
                o_copy(piece, bunch, k).start()

    for piece in range(cuts):
        place(piece, hp, obuf[piece].at[hp])

    for o in offsets:
        i_copy(o).wait_send()
        k_copy(o).wait_send()
        k_forward(reach - o, half).wait_send()
        for piece in range(cuts):
            v_copy(o, piece).wait_send()
            v_forward(reach - o, piece, half).wait_send()

    for piece in range(cuts):
        for k in range(1, n_head):
            source = lax.rem(hp - k + n_head, n_head)
            for bunch in range(BUNCHES):
                o_copy(piece, bunch, k).wait_recv()
            place(piece, source, stage[piece].at[source])
    for piece in range(cuts):
        for k in range(1, n_head):
            for bunch in range(BUNCHES):
                o_copy(piece, bunch, k).wait_send()


def on_device(queries, positions, key_codes, value_codes, scale_index, scale_table, block_lists):
    n_ctx = lax.axis_size("ctx")
    n_head = lax.axis_size("head")
    reach = min(3, (n_ctx - 1) // 2)
    rows, heads, dh = queries.shape
    keys = key_codes.shape[1]
    kblocks = keys // BLOCK
    coded = key_codes.reshape(key_codes.shape[0], kblocks, BLOCK, dh)
    nsel = block_lists.shape[2]
    slots = 2 * reach + 1
    assert rows == BLOCK and n_head % 2 == 0 and GROUP % (2 * heads) == 0
    exponents = -2.0 * np.repeat(np.arange(dh // 2), 2) / dh
    freq = jnp.asarray((ROPE_BASE**exponents).astype(np.float32)[None, :])
    bf16, f32 = jnp.bfloat16, jnp.float32
    dma = pltpu.SemaphoreType.DMA
    hbm = pl.BlockSpec(memory_space=pltpu.HBM)
    return pl.pallas_call(
        functools.partial(attend, reach, n_ctx, n_head),
        out_shape=pltpu.VMEM((rows // n_head, n_head * heads * dh), bf16),
        in_specs=[hbm] * 8,
        out_specs=pl.BlockSpec(memory_space=pltpu.VMEM),
        scratch_shapes=[
            pltpu.SMEM(block_lists.shape, jnp.int32),
            pltpu.SMEM((slots,) + scale_index.shape, jnp.int32),
            pltpu.SMEM(scale_table.shape, f32),
            pltpu.VMEM((1, rows), jnp.int32),
            pltpu.VMEM((1, dh), f32),
            pltpu.VMEM((rows * heads, dh), bf16),
            pltpu.VMEM((slots, kblocks, BLOCK, dh), bf16),
            pltpu.VMEM((keys, dh), bf16),
            pltpu.VMEM((rows * heads, dh), f32),
            pltpu.VMEM((heads, rows, dh), bf16),
            pltpu.VMEM((slots * kblocks, BLOCK, dh), bf16),
            [pltpu.VMEM((slots * kblocks, dh // cut, BLOCK), bf16) for cut in CUTS],
            pltpu.VMEM((heads, nsel * BLOCK, rows), bf16),
            pltpu.VMEM((heads, 1, rows), f32),
            [pltpu.VMEM((n_head, heads // cut, rows // n_head, dh), bf16) for cut in CUTS],
            [pltpu.VMEM((n_head, heads // cut, rows // n_head, dh), bf16) for cut in CUTS],
            dma((8,)),
            dma((slots,)),
            dma((slots,)),
            dma((slots,)),
            dma((slots,)),
            dma((slots, len(CUTS))),
            dma((slots, len(CUTS))),
            dma((slots,)),
            dma((slots,)),
            dma((slots, len(CUTS))),
            dma((slots, len(CUTS))),
            dma((len(CUTS), BUNCHES, n_head - 1)),
            dma((len(CUTS), BUNCHES, n_head - 1)),
            pltpu.SemaphoreType.REGULAR((slots,)),
            pltpu.SemaphoreType.REGULAR((n_head - 1,)),
        ],
        compiler_params=pltpu.CompilerParams(
            collective_id=0, has_side_effects=True, vmem_limit_bytes=67043328 - 2 * rows * heads * dh
        ),
        name="attend",
    )(
        block_lists,
        scale_index,
        scale_table,
        positions.reshape(1, rows),
        freq,
        queries.reshape(rows * heads, dh),
        coded,
        value_codes,
    )


def solution(mesh):
    placed = (
        P(("groups", "ctx"), "head", None),
        P(("groups", "ctx")),
        P("groups", "ctx", None),
        P("groups", "ctx", None),
        P("groups", None, "ctx"),
        P(),
        P(("groups", "head"), None, None),
    )
    return jax.shard_map(
        on_device,
        mesh=mesh,
        in_specs=placed,
        out_specs=P(("groups", "ctx", "head"), None),
        check_vma=False,
    )
```

```python
import functools
import math

import jax
import jax.numpy as jnp
import numpy as np
from jax import lax
from jax.experimental import pallas as pl
from jax.experimental.pallas import tpu as pltpu
from jax.sharding import PartitionSpec as P

GROUP = 16
BLOCK = 128
ROPE_BASE = 500000.0
CUTS = (2, 2)
BUNCHES = 1
MESH = pl.DeviceIdType.MESH


def attend(
    reach, n_ctx, n_head,
    lists_hbm, index_hbm, table_hbm, pos_hbm, freq_hbm, q_hbm, k_hbm, v_hbm,
    out_ref,
    lists_s, index_s, table_s, pos_ref, freq_ref,
    qcode, kcode, vcode, qwide, qrot, kbuf, vbuf, wbuf, lbuf, obuf, stage,
    load_sem, isend, irecv, ksend, krecv, vsend, vrecv, kfs, kfr, vfs, vfr, osend, orecv,
    ctx_in, head_in, row_in,
):
    c = lax.axis_index("ctx")
    hp = lax.axis_index("head")
    heads, rows, dh = qrot.shape
    kblocks = kcode.shape[1]
    nsel = lists_s.shape[2]
    rows_per = out_ref.shape[0]
    slots = 2 * reach + 1
    half = lax.rem(hp, 2)
    sib = hp + 1 - 2 * half
    kv_head = hp * heads // GROUP

    offsets = [o for d in range(1, reach + 1) for o in (d, -d)]
    others = range(1, n_head)

    def ctx_of(o):
        return lax.rem(c + o + n_ctx, n_ctx)

    def head_of(k):
        return lax.rem(hp + k, n_head)

    def rank(h):
        return n_head - 1 - h

    def direct(k):
        return jnp.logical_or(c == 0, head_of(k) == sib)

    barrier = pltpu.get_barrier_semaphore()
    greeted = jnp.int32(0)
    for o in offsets:
        greeted += (ctx_of(o) < c).astype(jnp.int32)

        @pl.when(ctx_of(o) > c)
        def _():
            pl.semaphore_signal(barrier, inc=1, device_id={"ctx": ctx_of(o)}, device_id_type=MESH)

    for k in others:
        greeted += jnp.logical_and(direct(k), rank(head_of(k)) < rank(hp)).astype(jnp.int32)

        @pl.when(jnp.logical_and(direct(k), rank(head_of(k)) > rank(hp)))
        def _():
            pl.semaphore_signal(barrier, inc=1, device_id={"head": head_of(k)}, device_id_type=MESH)

    k_load = pltpu.make_async_copy(k_hbm.at[kv_head], kcode.at[reach], load_sem.at[0])
    v_load = pltpu.make_async_copy(v_hbm.at[kv_head], vcode, load_sem.at[1])
    q_load = pltpu.make_async_copy(q_hbm, qcode, load_sem.at[2])
    small = [
        pltpu.make_async_copy(src, dst, load_sem.at[3 + i])
        for i, (src, dst) in enumerate(
            [
                (index_hbm, index_s.at[reach]),
                (table_hbm, table_s),
                (lists_hbm, lists_s),
                (pos_hbm, pos_ref),
                (freq_hbm, freq_ref),
            ]
        )
    ]
    v_load.start()
    for copy in small:
        copy.start()
    k_load.start()
    q_load.start()

    own = reach * kblocks
    part = kblocks // 2
    cuts = len(vbuf)
    wides = [ref.shape[1] for ref in vbuf]
    firsts = [sum(wides[:piece]) for piece in range(cuts)]

    def i_copy(o):
        return pltpu.make_async_remote_copy(
            src_ref=index_hbm,
            dst_ref=index_s.at[reach - o],
            send_sem=isend.at[reach - o],
            recv_sem=irecv.at[reach - o],
            device_id={"ctx": ctx_of(o)},
            device_id_type=MESH,
        )

    def k_copy(o):
        return pltpu.make_async_remote_copy(
            src_ref=k_hbm.at[kv_head, pl.ds(half * part, part)],
            dst_ref=kcode.at[reach - o, pl.ds(half * part, part)],
            send_sem=ksend.at[reach - o],
            recv_sem=krecv.at[reach - o],
            device_id={"ctx": ctx_of(o)},
            device_id_type=MESH,
        )

    def v_copy(o, piece):
        return pltpu.make_async_remote_copy(
            src_ref=vbuf[piece].at[pl.ds(own + half * part, part)],
            dst_ref=vbuf[piece].at[
                pl.ds((reach - o) * kblocks + half * part, part)
            ],
            send_sem=vsend.at[reach - o, piece],
            recv_sem=vrecv.at[reach - o, piece],
            device_id={"ctx": ctx_of(o)},
            device_id_type=MESH,
        )

    def k_forward(slot, which):
        region = kcode.at[slot, pl.ds(which * part, part)]
        return forward(region, kfs.at[slot], kfr.at[slot])

    def v_forward(slot, piece, which):
        region = vbuf[piece].at[pl.ds(slot * kblocks + which * (part), part)]
        return forward(region, vfs.at[slot, piece], vfr.at[slot, piece])

    def forward(region, send, recv):
        return pltpu.make_async_remote_copy(
            src_ref=region,
            dst_ref=region,
            send_sem=send,
            recv_sem=recv,
            device_id={"head": sib},
            device_id_type=MESH,
        )

    def start_keys(o):
        k_copy(o).start()
        i_copy(o).start()

    def start_values(o):
        for piece in range(cuts):
            v_copy(o, piece).start()

    def start_value(piece, o):
        v_copy(o, piece).start()

    def on_core(which, order, lower, step):
        for o in order:
            side = ctx_of(o) < c if lower else ctx_of(o) > c
            pl.when(jnp.logical_and(half == which, side))(functools.partial(step, o))

    @pl.when(greeted > 0)
    def _():
        pl.semaphore_wait(barrier, greeted)

    on_core(0, offsets, True, start_keys)
    on_core(1, offsets, True, start_keys)
    for o in offsets:

        @pl.when(ctx_of(o) < c)
        def _():
            pl.semaphore_signal(
                ctx_in.at[reach - o], inc=1, device_id={"ctx": ctx_of(o)}, device_id_type=MESH
            )

    for k in others:

        @pl.when(jnp.logical_and(direct(k), rank(head_of(k)) < rank(hp)))
        def _():
            pl.semaphore_signal(
                head_in.at[n_head - k - 1], inc=1, device_id={"head": head_of(k)}, device_id_type=MESH
            )

    def greet_head(k):
        @pl.when(jnp.logical_or(jnp.logical_not(direct(k)), rank(head_of(k)) > rank(hp)))
        def _():
            pl.semaphore_wait(head_in.at[k - 1], 1)

    def tell_row(k):
        @pl.when(jnp.logical_and(c + 1 < n_ctx, head_of(k) != sib))
        def _():
            pl.semaphore_signal(
                row_in.at[n_head - k - 1], inc=1, device_id={"head": head_of(k)}, device_id_type=MESH
            )

    def tell_next(k):
        @pl.when(jnp.logical_and(c + 1 < n_ctx, head_of(k) != sib))
        def _():
            pl.semaphore_wait(row_in.at[k - 1], 1)
            pl.semaphore_signal(
                head_in.at[k - 1], inc=1, device_id={"ctx": ctx_of(1)}, device_id_type=MESH
            )

    def scale_key(slot, b):
        s = table_s[0, index_s[slot, 0, kv_head, b]]
        kbuf[slot * kblocks + b] = (kcode[slot, b].astype(jnp.float32) * s).astype(jnp.bfloat16)

    v_load.wait()
    for copy in small[:2]:
        copy.wait()
    for b in range(kblocks):
        s = table_s[1, index_s[reach, 1, kv_head, b]]
        rounded = (vcode[b * BLOCK : (b + 1) * BLOCK, :].astype(jnp.float32) * s).astype(jnp.bfloat16)
        turned = rounded.astype(jnp.float32).T
        for piece in range(cuts):
            first, wide = firsts[piece], wides[piece]
            vbuf[piece][own + b] = turned[first : first + wide, :].astype(jnp.bfloat16)
    on_core(0, offsets, True, start_values)
    on_core(1, offsets, True, start_values)

    k_load.wait()
    for b in range(kblocks):
        scale_key(reach, b)

    def greet_keys(o):
        pl.semaphore_wait(ctx_in.at[reach + o], 1)
        start_keys(o)

    def greet_both(o):
        greet_keys(o)
        start_values(o)

    on_core(0, offsets, False, greet_keys)
    on_core(1, offsets, False, greet_keys)
    for piece in range(cuts):
        on_core(0, offsets, False, functools.partial(start_value, piece))
        on_core(1, offsets, False, functools.partial(start_value, piece))

    q_load.wait()
    for copy in small[2:]:
        copy.wait()
    qwide[...] = qcode[...].astype(jnp.float32)
    pos = jnp.broadcast_to(pos_ref[...].astype(jnp.float32), (rows, rows)).T
    angle = pos * freq_ref[...]
    lane = lax.broadcasted_iota(jnp.int32, (rows, dh), 1)
    even = lax.rem(lane, 2) == 0
    cosine = jnp.cos(angle)
    sine = jnp.sin(angle)
    sine = jnp.where(even, -sine, sine)
    for h in range(heads):
        x = qwide[pl.ds(h, rows, stride=heads), :]
        other = jnp.where(even, pltpu.roll(x, dh - 1, 1), pltpu.roll(x, 1, 1))
        qrot[h] = (x * cosine + other * sine).astype(jnp.bfloat16)

    for step in (greet_head, tell_row, tell_next):
        for k in others:
            step(k)
    for o in offsets:
        k_copy(o).wait_recv()
        k_forward(reach - o, half).start()
        i_copy(o).wait_recv()
        for b in range(part):
            scale_key(reach - o, half * part + b)
    for o in offsets:
        k_forward(reach - o, 1 - half).wait_recv()
        for b in range(part):
            scale_key(reach - o, (1 - half) * part + b)

    total = n_ctx * kblocks
    base = total - (c - reach) * kblocks
    factor = math.log2(math.e) / math.sqrt(dh)

    def block_of(h, j):
        return jnp.minimum(lax.rem(lists_s[h, c, j] + base, total), slots * kblocks - 1)

    def score(h, carry):
        gathered = jnp.concatenate([kbuf[block_of(h, j)] for j in range(nsel)], axis=0)
        s = lax.dot_general(
            gathered, qrot[h], (((1,), (1,)), ((), ())), preferred_element_type=jnp.float32
        )
        m = jnp.max(s, axis=0, keepdims=True)
        w = jnp.exp2((s - m) * factor)
        lbuf[h] = 1.0 / jnp.sum(w, axis=0, keepdims=True)
        wbuf[h] = w.astype(jnp.bfloat16)
        return carry

    lax.fori_loop(0, heads, score, 0, unroll=True)

    def o_copy(piece, bunch, k):
        peer = head_of(k)
        size = obuf[piece].shape[1] // BUNCHES
        region = pl.ds(bunch * size, size)
        return pltpu.make_async_remote_copy(
            src_ref=obuf[piece].at[peer, region],
            dst_ref=stage[piece].at[hp, region],
            send_sem=osend.at[piece, bunch, k - 1],
            recv_sem=orecv.at[piece, bunch, k - 1],
            device_id={"head": peer},
            device_id_type=MESH,
        )

    def value(piece, g):
        pack = dh // wides[piece]
        parts = []
        for h in range(g * pack, (g + 1) * pack):
            gathered = jnp.concatenate([vbuf[piece][block_of(h, j)] for j in range(nsel)], axis=1)
            o = jnp.dot(gathered, wbuf[h], preferred_element_type=jnp.float32)
            parts.append(o * lbuf[h])
        t = jnp.concatenate(parts, axis=0).T
        for p in range(n_head):
            obuf[piece][p, g] = t[p * rows_per : (p + 1) * rows_per, :].astype(jnp.bfloat16)

    out_lane = lax.broadcasted_iota(jnp.int32, (rows_per, dh), 1)

    def place(piece, source, ref):
        first, wide = firsts[piece], wides[piece]
        pack = dh // wide
        ours = jnp.logical_and(out_lane >= first, out_lane < first + wide)
        for g in range(ref.shape[0]):
            tile = ref[g].astype(jnp.float32)
            for i in range(pack):
                where = pl.ds(pl.multiple_of((source * heads + g * pack + i) * dh, dh), dh)
                shift = (first - i * wide) % dh
                moved = pltpu.roll(tile, shift, 1) if shift else tile
                if piece:
                    moved = jnp.where(ours, moved, out_ref[:, where].astype(jnp.float32))
                out_ref[:, where] = moved.astype(jnp.bfloat16)

    def pass_on(piece):
        for o in offsets:
            v_copy(o, piece).wait_recv()
            v_forward(reach - o, piece, half).start()

    pass_on(0)
    for piece in range(cuts):
        if piece + 1 < cuts:
            pass_on(piece + 1)
        for o in offsets:
            v_forward(reach - o, piece, 1 - half).wait_recv()
        groups = obuf[piece].shape[1]
        for bunch in range(BUNCHES):
            for g in range(groups // BUNCHES * bunch, groups // BUNCHES * (bunch + 1)):
                value(piece, g)
            for k in others:
                o_copy(piece, bunch, k).start()

    for piece in range(cuts):
        place(piece, hp, obuf[piece].at[hp])

    for o in offsets:
        i_copy(o).wait_send()
        k_copy(o).wait_send()
        k_forward(reach - o, half).wait_send()
        for piece in range(cuts):
            v_copy(o, piece).wait_send()
            v_forward(reach - o, piece, half).wait_send()

    for piece in range(cuts):
        for k in range(1, n_head):
            source = lax.rem(hp - k + n_head, n_head)
            for bunch in range(BUNCHES):
                o_copy(piece, bunch, k).wait_recv()
            place(piece, source, stage[piece].at[source])
    for piece in range(cuts):
        for k in range(1, n_head):
            for bunch in range(BUNCHES):
                o_copy(piece, bunch, k).wait_send()


def on_device(queries, positions, key_codes, value_codes, scale_index, scale_table, block_lists):
    n_ctx = lax.axis_size("ctx")
    n_head = lax.axis_size("head")
    reach = min(3, (n_ctx - 1) // 2)
    rows, heads, dh = queries.shape
    keys = key_codes.shape[1]
    kblocks = keys // BLOCK
    coded = key_codes.reshape(key_codes.shape[0], kblocks, BLOCK, dh)
    nsel = block_lists.shape[2]
    slots = 2 * reach + 1
    assert rows == BLOCK and n_head % 2 == 0 and GROUP % (2 * heads) == 0
    exponents = -2.0 * np.repeat(np.arange(dh // 2), 2) / dh
    freq = jnp.asarray((ROPE_BASE**exponents).astype(np.float32)[None, :])
    bf16, f32 = jnp.bfloat16, jnp.float32
    dma = pltpu.SemaphoreType.DMA
    hbm = pl.BlockSpec(memory_space=pltpu.HBM)
    return pl.pallas_call(
        functools.partial(attend, reach, n_ctx, n_head),
        out_shape=pltpu.VMEM((rows // n_head, n_head * heads * dh), bf16),
        in_specs=[hbm] * 8,
        out_specs=pl.BlockSpec(memory_space=pltpu.VMEM),
        scratch_shapes=[
            pltpu.SMEM(block_lists.shape, jnp.int32),
            pltpu.SMEM((slots,) + scale_index.shape, jnp.int32),
            pltpu.SMEM(scale_table.shape, f32),
            pltpu.VMEM((1, rows), jnp.int32),
            pltpu.VMEM((1, dh), f32),
            pltpu.VMEM((rows * heads, dh), bf16),
            pltpu.VMEM((slots, kblocks, BLOCK, dh), bf16),
            pltpu.VMEM((keys, dh), bf16),
            pltpu.VMEM((rows * heads, dh), f32),
            pltpu.VMEM((heads, rows, dh), bf16),
            pltpu.VMEM((slots * kblocks, BLOCK, dh), bf16),
            [pltpu.VMEM((slots * kblocks, dh // cut, BLOCK), bf16) for cut in CUTS],
            pltpu.VMEM((heads, nsel * BLOCK, rows), bf16),
            pltpu.VMEM((heads, 1, rows), f32),
            [pltpu.VMEM((n_head, heads // cut, rows // n_head, dh), bf16) for cut in CUTS],
            [pltpu.VMEM((n_head, heads // cut, rows // n_head, dh), bf16) for cut in CUTS],
            dma((8,)),
            dma((slots,)),
            dma((slots,)),
            dma((slots,)),
            dma((slots,)),
            dma((slots, len(CUTS))),
            dma((slots, len(CUTS))),
            dma((slots,)),
            dma((slots,)),
            dma((slots, len(CUTS))),
            dma((slots, len(CUTS))),
            dma((len(CUTS), BUNCHES, n_head - 1)),
            dma((len(CUTS), BUNCHES, n_head - 1)),
            pltpu.SemaphoreType.REGULAR((slots,)),
            pltpu.SemaphoreType.REGULAR((n_head - 1,)),
            pltpu.SemaphoreType.REGULAR((n_head - 1,)),
        ],
        compiler_params=pltpu.CompilerParams(
            collective_id=0, has_side_effects=True, vmem_limit_bytes=67043328 - 2 * rows * heads * dh
        ),
        name="attend",
    )(
        block_lists,
        scale_index,
        scale_table,
        positions.reshape(1, rows),
        freq,
        queries.reshape(rows * heads, dh),
        coded,
        value_codes,
    )


def solution(mesh):
    placed = (
        P(("groups", "ctx"), "head", None),
        P(("groups", "ctx")),
        P("groups", "ctx", None),
        P("groups", "ctx", None),
        P("groups", None, "ctx"),
        P(),
        P(("groups", "head"), None, None),
    )
    return jax.shard_map(
        on_device,
        mesh=mesh,
        in_specs=placed,
        out_specs=P(("groups", "ctx", "head"), None),
        check_vma=False,
    )
```

```python
import functools
import math

import jax
import jax.numpy as jnp
import numpy as np
from jax import lax
from jax.experimental import pallas as pl
from jax.experimental.pallas import tpu as pltpu
from jax.sharding import PartitionSpec as P

GROUP = 16
BLOCK = 128
ROPE_BASE = 500000.0
CUTS = (2, 2)
BUNCHES = 1
MESH = pl.DeviceIdType.MESH


def attend(
    reach, n_ctx, n_head,
    lists_hbm, index_hbm, table_hbm, pos_hbm, freq_hbm, q_hbm, k_hbm, v_hbm,
    out_ref,
    lists_s, index_s, table_s, pos_ref, freq_ref,
    qcode, kcode, vcode, qwide, qrot, kbuf, vbuf, wbuf, lbuf, obuf, stage,
    load_sem, isend, irecv, ksend, krecv, vsend, vrecv, kfs, kfr, vfs, vfr, osend, orecv,
    ctx_in, head_in, row_in,
):
    c = lax.axis_index("ctx")
    hp = lax.axis_index("head")
    heads, rows, dh = qrot.shape
    kblocks = kcode.shape[1]
    nsel = lists_s.shape[2]
    rows_per = out_ref.shape[0]
    slots = 2 * reach + 1
    half = lax.rem(hp, 2)
    sib = hp + 1 - 2 * half
    kv_head = hp * heads // GROUP

    offsets = [o for d in range(1, reach + 1) for o in (d, -d)]
    others = range(1, n_head)

    def ctx_of(o):
        return lax.rem(c + o + n_ctx, n_ctx)

    def head_of(k):
        return lax.rem(hp + k, n_head)

    def rank(h):
        return n_head - 1 - h

    def direct(k):
        return jnp.logical_or(c == 0, head_of(k) == sib)

    barrier = pltpu.get_barrier_semaphore()
    greeted = jnp.int32(0)
    for o in offsets:
        greeted += (ctx_of(o) < c).astype(jnp.int32)

        @pl.when(ctx_of(o) > c)
        def _():
            pl.semaphore_signal(barrier, inc=1, device_id={"ctx": ctx_of(o)}, device_id_type=MESH)

    for k in others:
        greeted += jnp.logical_and(direct(k), rank(head_of(k)) < rank(hp)).astype(jnp.int32)

        @pl.when(jnp.logical_and(direct(k), rank(head_of(k)) > rank(hp)))
        def _():
            pl.semaphore_signal(barrier, inc=1, device_id={"head": head_of(k)}, device_id_type=MESH)

    k_load = pltpu.make_async_copy(k_hbm.at[kv_head], kcode.at[reach], load_sem.at[0])
    v_load = pltpu.make_async_copy(v_hbm.at[kv_head], vcode, load_sem.at[1])
    q_load = pltpu.make_async_copy(q_hbm, qcode, load_sem.at[2])
    small = [
        pltpu.make_async_copy(src, dst, load_sem.at[3 + i])
        for i, (src, dst) in enumerate(
            [
                (index_hbm, index_s.at[reach]),
                (table_hbm, table_s),
                (lists_hbm, lists_s),
                (pos_hbm, pos_ref),
                (freq_hbm, freq_ref),
            ]
        )
    ]
    v_load.start()
    for copy in small:
        copy.start()
    k_load.start()
    q_load.start()

    own = reach * kblocks
    part = kblocks // 2
    cuts = len(vbuf)
    wides = [ref.shape[1] for ref in vbuf]
    firsts = [sum(wides[:piece]) for piece in range(cuts)]

    def i_copy(o):
        return pltpu.make_async_remote_copy(
            src_ref=index_hbm,
            dst_ref=index_s.at[reach - o],
            send_sem=isend.at[reach - o],
            recv_sem=irecv.at[reach - o],
            device_id={"ctx": ctx_of(o)},
            device_id_type=MESH,
        )

    def k_copy(o):
        return pltpu.make_async_remote_copy(
            src_ref=k_hbm.at[kv_head, pl.ds(half * part, part)],
            dst_ref=kcode.at[reach - o, pl.ds(half * part, part)],
            send_sem=ksend.at[reach - o],
            recv_sem=krecv.at[reach - o],
            device_id={"ctx": ctx_of(o)},
            device_id_type=MESH,
        )

    def v_copy(o, piece):
        return pltpu.make_async_remote_copy(
            src_ref=vbuf[piece].at[pl.ds(own + half * part, part)],
            dst_ref=vbuf[piece].at[
                pl.ds((reach - o) * kblocks + half * part, part)
            ],
            send_sem=vsend.at[reach - o, piece],
            recv_sem=vrecv.at[reach - o, piece],
            device_id={"ctx": ctx_of(o)},
            device_id_type=MESH,
        )

    def k_forward(slot, which):
        region = kcode.at[slot, pl.ds(which * part, part)]
        return forward(region, kfs.at[slot], kfr.at[slot])

    def v_forward(slot, piece, which):
        region = vbuf[piece].at[pl.ds(slot * kblocks + which * (part), part)]
        return forward(region, vfs.at[slot, piece], vfr.at[slot, piece])

    def forward(region, send, recv):
        return pltpu.make_async_remote_copy(
            src_ref=region,
            dst_ref=region,
            send_sem=send,
            recv_sem=recv,
            device_id={"head": sib},
            device_id_type=MESH,
        )

    def start_keys(o):
        k_copy(o).start()
        i_copy(o).start()

    def start_values(o):
        for piece in range(cuts):
            v_copy(o, piece).start()

    def start_value(piece, o):
        v_copy(o, piece).start()

    def on_core(which, order, lower, step):
        for o in order:
            side = ctx_of(o) < c if lower else ctx_of(o) > c
            pl.when(jnp.logical_and(half == which, side))(functools.partial(step, o))

    @pl.when(greeted > 0)
    def _():
        pl.semaphore_wait(barrier, greeted)

    on_core(0, offsets, True, start_keys)
    on_core(1, offsets, True, start_keys)
    for o in offsets:

        @pl.when(ctx_of(o) < c)
        def _():
            pl.semaphore_signal(
                ctx_in.at[reach - o], inc=1, device_id={"ctx": ctx_of(o)}, device_id_type=MESH
            )

    for k in others:

        @pl.when(jnp.logical_and(direct(k), rank(head_of(k)) < rank(hp)))
        def _():
            pl.semaphore_signal(
                head_in.at[n_head - k - 1], inc=1, device_id={"head": head_of(k)}, device_id_type=MESH
            )

    def greet_head(k):
        @pl.when(jnp.logical_or(jnp.logical_not(direct(k)), rank(head_of(k)) > rank(hp)))
        def _():
            pl.semaphore_wait(head_in.at[k - 1], 1)

    def tell_row(k):
        @pl.when(jnp.logical_and(c + 1 < n_ctx, head_of(k) != sib))
        def _():
            pl.semaphore_signal(
                row_in.at[n_head - k - 1], inc=1, device_id={"head": head_of(k)}, device_id_type=MESH
            )

    def tell_next(k):
        @pl.when(jnp.logical_and(c + 1 < n_ctx, head_of(k) != sib))
        def _():
            pl.semaphore_wait(row_in.at[k - 1], 1)
            pl.semaphore_signal(
                head_in.at[k - 1], inc=1, device_id={"ctx": ctx_of(1)}, device_id_type=MESH
            )

    def scale_key(slot, b):
        s = table_s[0, index_s[slot, 0, kv_head, b]]
        kbuf[slot * kblocks + b] = (kcode[slot, b].astype(jnp.float32) * s).astype(jnp.bfloat16)

    v_load.wait()
    for copy in small[:2]:
        copy.wait()
    for b in range(kblocks):
        s = table_s[1, index_s[reach, 1, kv_head, b]]
        rounded = (vcode[b * BLOCK : (b + 1) * BLOCK, :].astype(jnp.float32) * s).astype(jnp.bfloat16)
        turned = rounded.astype(jnp.float32).T
        for piece in range(cuts):
            first, wide = firsts[piece], wides[piece]
            vbuf[piece][own + b] = turned[first : first + wide, :].astype(jnp.bfloat16)
    on_core(0, offsets, True, start_values)
    on_core(1, offsets, True, start_values)

    k_load.wait()
    for b in range(kblocks):
        scale_key(reach, b)

    def greet_keys(o):
        pl.semaphore_wait(ctx_in.at[reach + o], 1)
        start_keys(o)

    def greet_both(o):
        greet_keys(o)
        start_values(o)

    on_core(0, offsets, False, greet_keys)
    on_core(1, offsets, False, greet_keys)
    for piece in range(cuts):
        on_core(0, offsets, False, functools.partial(start_value, piece))
        on_core(1, offsets, False, functools.partial(start_value, piece))

    q_load.wait()
    for copy in small[2:]:
        copy.wait()
    qwide[...] = qcode[...].astype(jnp.float32)
    pos = jnp.broadcast_to(pos_ref[...].astype(jnp.float32), (rows, rows)).T
    angle = pos * freq_ref[...]
    lane = lax.broadcasted_iota(jnp.int32, (rows, dh), 1)
    even = lax.rem(lane, 2) == 0
    cosine = jnp.cos(angle)
    sine = jnp.sin(angle)
    sine = jnp.where(even, -sine, sine)
    for h in range(heads):
        x = qwide[pl.ds(h, rows, stride=heads), :]
        other = jnp.where(even, pltpu.roll(x, dh - 1, 1), pltpu.roll(x, 1, 1))
        qrot[h] = (x * cosine + other * sine).astype(jnp.bfloat16)

    for step in (greet_head, tell_row, tell_next):
        for k in others:
            step(k)
    for o in offsets:
        k_copy(o).wait_recv()
        k_forward(reach - o, half).start()
        i_copy(o).wait_recv()
        for b in range(part):
            scale_key(reach - o, half * part + b)
    for o in offsets:
        k_forward(reach - o, 1 - half).wait_recv()
        for b in range(part):
            scale_key(reach - o, (1 - half) * part + b)

    total = n_ctx * kblocks
    base = total - (c - reach) * kblocks
    factor = math.log2(math.e) / math.sqrt(dh)

    def block_of(h, j):
        return jnp.minimum(lax.rem(lists_s[h, c, j] + base, total), slots * kblocks - 1)

    def score(h, carry):
        gathered = jnp.concatenate([kbuf[block_of(h, j)] for j in range(nsel)], axis=0)
        s = lax.dot_general(
            gathered, qrot[h], (((1,), (1,)), ((), ())), preferred_element_type=jnp.float32
        )
        m = jnp.max(s, axis=0, keepdims=True)
        w = jnp.exp2((s - m) * factor)
        lbuf[h] = 1.0 / jnp.sum(w, axis=0, keepdims=True)
        wbuf[h] = w.astype(jnp.bfloat16)
        return carry

    lax.fori_loop(0, heads, score, 0, unroll=True)

    def o_copy(piece, bunch, k):
        peer = head_of(k)
        size = obuf[piece].shape[1] // BUNCHES
        region = pl.ds(bunch * size, size)
        return pltpu.make_async_remote_copy(
            src_ref=obuf[piece].at[peer, region],
            dst_ref=stage[piece].at[hp, region],
            send_sem=osend.at[piece, bunch, k - 1],
            recv_sem=orecv.at[piece, bunch, k - 1],
            device_id={"head": peer},
            device_id_type=MESH,
        )

    def value(piece, g):
        pack = dh // wides[piece]
        parts = []
        for h in range(g * pack, (g + 1) * pack):
            gathered = jnp.concatenate([vbuf[piece][block_of(h, j)] for j in range(nsel)], axis=1)
            o = jnp.dot(gathered, wbuf[h], preferred_element_type=jnp.float32)
            parts.append(o * lbuf[h])
        t = jnp.concatenate(parts, axis=0).T
        for p in range(n_head):
            obuf[piece][p, g] = t[p * rows_per : (p + 1) * rows_per, :].astype(jnp.bfloat16)

    out_lane = lax.broadcasted_iota(jnp.int32, (rows_per, dh), 1)

    def place(piece, source, ref):
        first, wide = firsts[piece], wides[piece]
        pack = dh // wide
        ours = jnp.logical_and(out_lane >= first, out_lane < first + wide)
        for g in range(ref.shape[0]):
            tile = ref[g].astype(jnp.float32)
            for i in range(pack):
                where = pl.ds(pl.multiple_of((source * heads + g * pack + i) * dh, dh), dh)
                shift = (first - i * wide) % dh
                moved = pltpu.roll(tile, shift, 1) if shift else tile
                if piece:
                    moved = jnp.where(ours, moved, out_ref[:, where].astype(jnp.float32))
                out_ref[:, where] = moved.astype(jnp.bfloat16)

    def pass_on(piece):
        for o in offsets:
            v_copy(o, piece).wait_recv()
            v_forward(reach - o, piece, half).start()

    pass_on(0)
    for piece in range(cuts):
        if piece + 1 < cuts:
            pass_on(piece + 1)
        for o in offsets:
            v_forward(reach - o, piece, 1 - half).wait_recv()
        groups = obuf[piece].shape[1]
        for bunch in range(BUNCHES):
            for g in range(groups // BUNCHES * bunch, groups // BUNCHES * (bunch + 1)):
                value(piece, g)
            for k in others:
                o_copy(piece, bunch, k).start()

    for piece in range(cuts):
        place(piece, hp, obuf[piece].at[hp])

    for o in offsets:
        i_copy(o).wait_send()
        k_copy(o).wait_send()
        k_forward(reach - o, half).wait_send()
        for piece in range(cuts):
            v_copy(o, piece).wait_send()
            v_forward(reach - o, piece, half).wait_send()

    for piece in range(cuts):
        for turn in range(n_head - 1):
            k = 1 + lax.rem(turn + (n_head - 2) * (1 - half), n_head - 1)
            source = lax.rem(hp - k + n_head, n_head)
            for bunch in range(BUNCHES):
                o_copy(piece, bunch, k).wait_recv()
            place(piece, source, stage[piece].at[source])
    for piece in range(cuts):
        for k in range(1, n_head):
            for bunch in range(BUNCHES):
                o_copy(piece, bunch, k).wait_send()


def on_device(queries, positions, key_codes, value_codes, scale_index, scale_table, block_lists):
    n_ctx = lax.axis_size("ctx")
    n_head = lax.axis_size("head")
    reach = min(3, (n_ctx - 1) // 2)
    rows, heads, dh = queries.shape
    keys = key_codes.shape[1]
    kblocks = keys // BLOCK
    coded = key_codes.reshape(key_codes.shape[0], kblocks, BLOCK, dh)
    nsel = block_lists.shape[2]
    slots = 2 * reach + 1
    assert rows == BLOCK and n_head % 2 == 0 and GROUP % (2 * heads) == 0
    exponents = -2.0 * np.repeat(np.arange(dh // 2), 2) / dh
    freq = jnp.asarray((ROPE_BASE**exponents).astype(np.float32)[None, :])
    bf16, f32 = jnp.bfloat16, jnp.float32
    dma = pltpu.SemaphoreType.DMA
    hbm = pl.BlockSpec(memory_space=pltpu.HBM)
    return pl.pallas_call(
        functools.partial(attend, reach, n_ctx, n_head),
        out_shape=pltpu.VMEM((rows // n_head, n_head * heads * dh), bf16),
        in_specs=[hbm] * 8,
        out_specs=pl.BlockSpec(memory_space=pltpu.VMEM),
        scratch_shapes=[
            pltpu.SMEM(block_lists.shape, jnp.int32),
            pltpu.SMEM((slots,) + scale_index.shape, jnp.int32),
            pltpu.SMEM(scale_table.shape, f32),
            pltpu.VMEM((1, rows), jnp.int32),
            pltpu.VMEM((1, dh), f32),
            pltpu.VMEM((rows * heads, dh), bf16),
            pltpu.VMEM((slots, kblocks, BLOCK, dh), bf16),
            pltpu.VMEM((keys, dh), bf16),
            pltpu.VMEM((rows * heads, dh), f32),
            pltpu.VMEM((heads, rows, dh), bf16),
            pltpu.VMEM((slots * kblocks, BLOCK, dh), bf16),
            [pltpu.VMEM((slots * kblocks, dh // cut, BLOCK), bf16) for cut in CUTS],
            pltpu.VMEM((heads, nsel * BLOCK, rows), bf16),
            pltpu.VMEM((heads, 1, rows), f32),
            [pltpu.VMEM((n_head, heads // cut, rows // n_head, dh), bf16) for cut in CUTS],
            [pltpu.VMEM((n_head, heads // cut, rows // n_head, dh), bf16) for cut in CUTS],
            dma((8,)),
            dma((slots,)),
            dma((slots,)),
            dma((slots,)),
            dma((slots,)),
            dma((slots, len(CUTS))),
            dma((slots, len(CUTS))),
            dma((slots,)),
            dma((slots,)),
            dma((slots, len(CUTS))),
            dma((slots, len(CUTS))),
            dma((len(CUTS), BUNCHES, n_head - 1)),
            dma((len(CUTS), BUNCHES, n_head - 1)),
            pltpu.SemaphoreType.REGULAR((slots,)),
            pltpu.SemaphoreType.REGULAR((n_head - 1,)),
            pltpu.SemaphoreType.REGULAR((n_head - 1,)),
        ],
        compiler_params=pltpu.CompilerParams(
            collective_id=0, has_side_effects=True, vmem_limit_bytes=67043328 - 2 * rows * heads * dh
        ),
        name="attend",
    )(
        block_lists,
        scale_index,
        scale_table,
        positions.reshape(1, rows),
        freq,
        queries.reshape(rows * heads, dh),
        coded,
        value_codes,
    )


def solution(mesh):
    placed = (
        P(("groups", "ctx"), "head", None),
        P(("groups", "ctx")),
        P("groups", "ctx", None),
        P("groups", "ctx", None),
        P("groups", None, "ctx"),
        P(),
        P(("groups", "head"), None, None),
    )
    return jax.shard_map(
        on_device,
        mesh=mesh,
        in_specs=placed,
        out_specs=P(("groups", "ctx", "head"), None),
        check_vma=False,
    )
```

```python
import functools
import math

import jax
import jax.numpy as jnp
import numpy as np
from jax import lax
from jax.experimental import pallas as pl
from jax.experimental.pallas import tpu as pltpu
from jax.sharding import PartitionSpec as P

GROUP = 16
BLOCK = 128
ROPE_BASE = 500000.0
CUTS = (2, 2)
BUNCHES = 1
MESH = pl.DeviceIdType.MESH


def attend(
    reach, n_ctx, n_head,
    lists_hbm, index_hbm, table_hbm, pos_hbm, freq_hbm, q_hbm, k_hbm, v_hbm,
    out_ref,
    lists_s, index_s, table_s, pos_ref, freq_ref,
    qcode, kcode, vcode, qwide, qrot, kbuf, vbuf, wbuf, lbuf, obuf, stage,
    load_sem, isend, irecv, ksend, krecv, vsend, vrecv, kfs, kfr, vfs, vfr, osend, orecv,
    ctx_in, head_in, row_in,
):
    c = lax.axis_index("ctx")
    hp = lax.axis_index("head")
    heads, rows, dh = qrot.shape
    kblocks = kcode.shape[1]
    nsel = lists_s.shape[2]
    rows_per = out_ref.shape[0]
    slots = 2 * reach + 1
    half = lax.rem(hp, 2)
    sib = hp + 1 - 2 * half
    kv_head = hp * heads // GROUP

    offsets = [o for d in range(1, reach + 1) for o in (d, -d)]
    others = range(1, n_head)

    def ctx_of(o):
        return lax.rem(c + o + n_ctx, n_ctx)

    def head_of(k):
        return lax.rem(hp + k, n_head)

    def rank(h):
        return n_head - 1 - h

    def direct(k):
        return jnp.logical_or(c == 0, head_of(k) == sib)

    barrier = pltpu.get_barrier_semaphore()
    greeted = jnp.int32(0)
    for o in offsets:
        greeted += (ctx_of(o) < c).astype(jnp.int32)

        @pl.when(ctx_of(o) > c)
        def _():
            pl.semaphore_signal(barrier, inc=1, device_id={"ctx": ctx_of(o)}, device_id_type=MESH)

    for k in others:
        greeted += jnp.logical_and(direct(k), rank(head_of(k)) < rank(hp)).astype(jnp.int32)

        @pl.when(jnp.logical_and(direct(k), rank(head_of(k)) > rank(hp)))
        def _():
            pl.semaphore_signal(barrier, inc=1, device_id={"head": head_of(k)}, device_id_type=MESH)

    k_load = pltpu.make_async_copy(k_hbm.at[kv_head], kcode.at[reach], load_sem.at[0])
    v_load = pltpu.make_async_copy(v_hbm.at[kv_head], vcode, load_sem.at[1])
    q_load = pltpu.make_async_copy(q_hbm, qcode, load_sem.at[2])
    small = [
        pltpu.make_async_copy(src, dst, load_sem.at[3 + i])
        for i, (src, dst) in enumerate(
            [
                (index_hbm, index_s.at[reach]),
                (table_hbm, table_s),
                (lists_hbm, lists_s),
                (pos_hbm, pos_ref),
                (freq_hbm, freq_ref),
            ]
        )
    ]
    v_load.start()
    for copy in small:
        copy.start()
    k_load.start()
    q_load.start()

    own = reach * kblocks
    part = kblocks // 2
    cuts = len(vbuf)
    wides = [ref.shape[1] for ref in vbuf]
    firsts = [sum(wides[:piece]) for piece in range(cuts)]

    def i_copy(o):
        return pltpu.make_async_remote_copy(
            src_ref=index_hbm,
            dst_ref=index_s.at[reach - o],
            send_sem=isend.at[reach - o],
            recv_sem=irecv.at[reach - o],
            device_id={"ctx": ctx_of(o)},
            device_id_type=MESH,
        )

    def k_copy(o):
        return pltpu.make_async_remote_copy(
            src_ref=k_hbm.at[kv_head, pl.ds(half * part, part)],
            dst_ref=kcode.at[reach - o, pl.ds(half * part, part)],
            send_sem=ksend.at[reach - o],
            recv_sem=krecv.at[reach - o],
            device_id={"ctx": ctx_of(o)},
            device_id_type=MESH,
        )

    def v_copy(o, piece):
        return pltpu.make_async_remote_copy(
            src_ref=vbuf[piece].at[pl.ds(own + half * part, part)],
            dst_ref=vbuf[piece].at[
                pl.ds((reach - o) * kblocks + half * part, part)
            ],
            send_sem=vsend.at[reach - o, piece],
            recv_sem=vrecv.at[reach - o, piece],
            device_id={"ctx": ctx_of(o)},
            device_id_type=MESH,
        )

    def k_forward(slot, which):
        region = kcode.at[slot, pl.ds(which * part, part)]
        return forward(region, kfs.at[slot], kfr.at[slot])

    def v_forward(slot, piece, which):
        region = vbuf[piece].at[pl.ds(slot * kblocks + which * (part), part)]
        return forward(region, vfs.at[slot, piece], vfr.at[slot, piece])

    def forward(region, send, recv):
        return pltpu.make_async_remote_copy(
            src_ref=region,
            dst_ref=region,
            send_sem=send,
            recv_sem=recv,
            device_id={"head": sib},
            device_id_type=MESH,
        )

    def start_keys(o):
        k_copy(o).start()
        i_copy(o).start()

    def start_values(o):
        for piece in range(cuts):
            v_copy(o, piece).start()

    def start_value(piece, o):
        v_copy(o, piece).start()

    def on_core(which, order, lower, step):
        for o in order:
            side = ctx_of(o) < c if lower else ctx_of(o) > c
            pl.when(jnp.logical_and(half == which, side))(functools.partial(step, o))

    @pl.when(greeted > 0)
    def _():
        pl.semaphore_wait(barrier, greeted)

    on_core(0, offsets, True, start_keys)
    on_core(1, offsets, True, start_keys)
    for o in offsets:

        @pl.when(ctx_of(o) < c)
        def _():
            pl.semaphore_signal(
                ctx_in.at[reach - o], inc=1, device_id={"ctx": ctx_of(o)}, device_id_type=MESH
            )

    for k in others:

        @pl.when(jnp.logical_and(direct(k), rank(head_of(k)) < rank(hp)))
        def _():
            pl.semaphore_signal(
                head_in.at[n_head - k - 1], inc=1, device_id={"head": head_of(k)}, device_id_type=MESH
            )

    def greet_head(k):
        @pl.when(jnp.logical_or(jnp.logical_not(direct(k)), rank(head_of(k)) > rank(hp)))
        def _():
            pl.semaphore_wait(head_in.at[k - 1], 1)

    def tell_row(k):
        @pl.when(jnp.logical_and(c + 1 < n_ctx, head_of(k) != sib))
        def _():
            pl.semaphore_signal(
                row_in.at[n_head - k - 1], inc=1, device_id={"head": head_of(k)}, device_id_type=MESH
            )

    def tell_next(k):
        @pl.when(jnp.logical_and(c + 1 < n_ctx, head_of(k) != sib))
        def _():
            pl.semaphore_wait(row_in.at[k - 1], 1)
            pl.semaphore_signal(
                head_in.at[k - 1], inc=1, device_id={"ctx": ctx_of(1)}, device_id_type=MESH
            )

    def scale_key(slot, b):
        s = table_s[0, index_s[slot, 0, kv_head, b]]
        kbuf[slot * kblocks + b] = (kcode[slot, b].astype(jnp.float32) * s).astype(jnp.bfloat16)

    v_load.wait()
    for copy in small[:2]:
        copy.wait()
    for b in range(kblocks):
        s = table_s[1, index_s[reach, 1, kv_head, b]]
        rounded = (vcode[b * BLOCK : (b + 1) * BLOCK, :].astype(jnp.float32) * s).astype(jnp.bfloat16)
        turned = rounded.astype(jnp.float32).T
        for piece in range(cuts):
            first, wide = firsts[piece], wides[piece]
            vbuf[piece][own + b] = turned[first : first + wide, :].astype(jnp.bfloat16)
    on_core(0, offsets, True, start_values)
    on_core(1, offsets, True, start_values)

    def greet_keys(o):
        pl.semaphore_wait(ctx_in.at[reach + o], 1)
        start_keys(o)

    def greet_both(o):
        greet_keys(o)
        start_values(o)

    on_core(0, offsets, False, greet_keys)
    on_core(1, offsets, False, greet_keys)
    for piece in range(cuts):
        on_core(0, offsets, False, functools.partial(start_value, piece))
        on_core(1, offsets, False, functools.partial(start_value, piece))

    k_load.wait()
    for b in range(kblocks):
        scale_key(reach, b)

    q_load.wait()
    for copy in small[2:]:
        copy.wait()
    qwide[...] = qcode[...].astype(jnp.float32)
    pos = jnp.broadcast_to(pos_ref[...].astype(jnp.float32), (rows, rows)).T
    angle = pos * freq_ref[...]
    lane = lax.broadcasted_iota(jnp.int32, (rows, dh), 1)
    even = lax.rem(lane, 2) == 0
    cosine = jnp.cos(angle)
    sine = jnp.sin(angle)
    sine = jnp.where(even, -sine, sine)
    for h in range(heads):
        x = qwide[pl.ds(h, rows, stride=heads), :]
        other = jnp.where(even, pltpu.roll(x, dh - 1, 1), pltpu.roll(x, 1, 1))
        qrot[h] = (x * cosine + other * sine).astype(jnp.bfloat16)

    for step in (greet_head, tell_row, tell_next):
        for k in others:
            step(k)
    for o in offsets:
        k_copy(o).wait_recv()
        k_forward(reach - o, half).start()
        i_copy(o).wait_recv()
        for b in range(part):
            scale_key(reach - o, half * part + b)
    for o in offsets:
        k_forward(reach - o, 1 - half).wait_recv()
        for b in range(part):
            scale_key(reach - o, (1 - half) * part + b)

    total = n_ctx * kblocks
    base = total - (c - reach) * kblocks
    factor = math.log2(math.e) / math.sqrt(dh)

    def block_of(h, j):
        return jnp.minimum(lax.rem(lists_s[h, c, j] + base, total), slots * kblocks - 1)

    def score(h, carry):
        gathered = jnp.concatenate([kbuf[block_of(h, j)] for j in range(nsel)], axis=0)
        s = lax.dot_general(
            gathered, qrot[h], (((1,), (1,)), ((), ())), preferred_element_type=jnp.float32
        )
        m = jnp.max(s, axis=0, keepdims=True)
        w = jnp.exp2((s - m) * factor)
        lbuf[h] = 1.0 / jnp.sum(w, axis=0, keepdims=True)
        wbuf[h] = w.astype(jnp.bfloat16)
        return carry

    lax.fori_loop(0, heads, score, 0, unroll=True)

    def o_copy(piece, bunch, k):
        peer = head_of(k)
        size = obuf[piece].shape[1] // BUNCHES
        region = pl.ds(bunch * size, size)
        return pltpu.make_async_remote_copy(
            src_ref=obuf[piece].at[peer, region],
            dst_ref=stage[piece].at[hp, region],
            send_sem=osend.at[piece, bunch, k - 1],
            recv_sem=orecv.at[piece, bunch, k - 1],
            device_id={"head": peer},
            device_id_type=MESH,
        )

    def value(piece, g):
        pack = dh // wides[piece]
        parts = []
        for h in range(g * pack, (g + 1) * pack):
            gathered = jnp.concatenate([vbuf[piece][block_of(h, j)] for j in range(nsel)], axis=1)
            o = jnp.dot(gathered, wbuf[h], preferred_element_type=jnp.float32)
            parts.append(o * lbuf[h])
        t = jnp.concatenate(parts, axis=0).T
        for p in range(n_head):
            obuf[piece][p, g] = t[p * rows_per : (p + 1) * rows_per, :].astype(jnp.bfloat16)

    out_lane = lax.broadcasted_iota(jnp.int32, (rows_per, dh), 1)

    def place(piece, source, ref):
        first, wide = firsts[piece], wides[piece]
        pack = dh // wide
        ours = jnp.logical_and(out_lane >= first, out_lane < first + wide)
        for g in range(ref.shape[0]):
            tile = ref[g].astype(jnp.float32)
            for i in range(pack):
                where = pl.ds(pl.multiple_of((source * heads + g * pack + i) * dh, dh), dh)
                shift = (first - i * wide) % dh
                moved = pltpu.roll(tile, shift, 1) if shift else tile
                if piece:
                    moved = jnp.where(ours, moved, out_ref[:, where].astype(jnp.float32))
                out_ref[:, where] = moved.astype(jnp.bfloat16)

    def pass_on(piece):
        for o in offsets:
            v_copy(o, piece).wait_recv()
            v_forward(reach - o, piece, half).start()

    pass_on(0)
    for piece in range(cuts):
        if piece + 1 < cuts:
            pass_on(piece + 1)
        for o in offsets:
            v_forward(reach - o, piece, 1 - half).wait_recv()
        groups = obuf[piece].shape[1]
        for bunch in range(BUNCHES):
            for g in range(groups // BUNCHES * bunch, groups // BUNCHES * (bunch + 1)):
                value(piece, g)
            for k in others:
                o_copy(piece, bunch, k).start()

    for piece in range(cuts):
        place(piece, hp, obuf[piece].at[hp])

    for o in offsets:
        i_copy(o).wait_send()
        k_copy(o).wait_send()
        k_forward(reach - o, half).wait_send()
        for piece in range(cuts):
            v_copy(o, piece).wait_send()
            v_forward(reach - o, piece, half).wait_send()

    for piece in range(cuts):
        for k in range(1, n_head):
            source = lax.rem(hp - k + n_head, n_head)
            for bunch in range(BUNCHES):
                o_copy(piece, bunch, k).wait_recv()
            place(piece, source, stage[piece].at[source])
    for piece in range(cuts):
        for k in range(1, n_head):
            for bunch in range(BUNCHES):
                o_copy(piece, bunch, k).wait_send()


def on_device(queries, positions, key_codes, value_codes, scale_index, scale_table, block_lists):
    n_ctx = lax.axis_size("ctx")
    n_head = lax.axis_size("head")
    reach = min(3, (n_ctx - 1) // 2)
    rows, heads, dh = queries.shape
    keys = key_codes.shape[1]
    kblocks = keys // BLOCK
    coded = key_codes.reshape(key_codes.shape[0], kblocks, BLOCK, dh)
    nsel = block_lists.shape[2]
    slots = 2 * reach + 1
    assert rows == BLOCK and n_head % 2 == 0 and GROUP % (2 * heads) == 0
    exponents = -2.0 * np.repeat(np.arange(dh // 2), 2) / dh
    freq = jnp.asarray((ROPE_BASE**exponents).astype(np.float32)[None, :])
    bf16, f32 = jnp.bfloat16, jnp.float32
    dma = pltpu.SemaphoreType.DMA
    hbm = pl.BlockSpec(memory_space=pltpu.HBM)
    return pl.pallas_call(
        functools.partial(attend, reach, n_ctx, n_head),
        out_shape=pltpu.VMEM((rows // n_head, n_head * heads * dh), bf16),
        in_specs=[hbm] * 8,
        out_specs=pl.BlockSpec(memory_space=pltpu.VMEM),
        scratch_shapes=[
            pltpu.SMEM(block_lists.shape, jnp.int32),
            pltpu.SMEM((slots,) + scale_index.shape, jnp.int32),
            pltpu.SMEM(scale_table.shape, f32),
            pltpu.VMEM((1, rows), jnp.int32),
            pltpu.VMEM((1, dh), f32),
            pltpu.VMEM((rows * heads, dh), bf16),
            pltpu.VMEM((slots, kblocks, BLOCK, dh), bf16),
            pltpu.VMEM((keys, dh), bf16),
            pltpu.VMEM((rows * heads, dh), f32),
            pltpu.VMEM((heads, rows, dh), bf16),
            pltpu.VMEM((slots * kblocks, BLOCK, dh), bf16),
            [pltpu.VMEM((slots * kblocks, dh // cut, BLOCK), bf16) for cut in CUTS],
            pltpu.VMEM((heads, nsel * BLOCK, rows), bf16),
            pltpu.VMEM((heads, 1, rows), f32),
            [pltpu.VMEM((n_head, heads // cut, rows // n_head, dh), bf16) for cut in CUTS],
            [pltpu.VMEM((n_head, heads // cut, rows // n_head, dh), bf16) for cut in CUTS],
            dma((8,)),
            dma((slots,)),
            dma((slots,)),
            dma((slots,)),
            dma((slots,)),
            dma((slots, len(CUTS))),
            dma((slots, len(CUTS))),
            dma((slots,)),
            dma((slots,)),
            dma((slots, len(CUTS))),
            dma((slots, len(CUTS))),
            dma((len(CUTS), BUNCHES, n_head - 1)),
            dma((len(CUTS), BUNCHES, n_head - 1)),
            pltpu.SemaphoreType.REGULAR((slots,)),
            pltpu.SemaphoreType.REGULAR((n_head - 1,)),
            pltpu.SemaphoreType.REGULAR((n_head - 1,)),
        ],
        compiler_params=pltpu.CompilerParams(
            collective_id=0, has_side_effects=True, vmem_limit_bytes=67043328 - 2 * rows * heads * dh
        ),
        name="attend",
    )(
        block_lists,
        scale_index,
        scale_table,
        positions.reshape(1, rows),
        freq,
        queries.reshape(rows * heads, dh),
        coded,
        value_codes,
    )


def solution(mesh):
    placed = (
        P(("groups", "ctx"), "head", None),
        P(("groups", "ctx")),
        P("groups", "ctx", None),
        P("groups", "ctx", None),
        P("groups", None, "ctx"),
        P(),
        P(("groups", "head"), None, None),
    )
    return jax.shard_map(
        on_device,
        mesh=mesh,
        in_specs=placed,
        out_specs=P(("groups", "ctx", "head"), None),
        check_vma=False,
    )
```
